256 devices in a mesh: rows: 32 (over x, z), cols: 4 (over y), space: 2 (over core).
Axes of the slice: x: 4, y: 4, z: 8, core: 2. Of those that a mesh axis runs over, the one named last changes fastest.
Arguments:
- hamiltonian: float32 [16384, 1536], P(('rows', 'cols', 'space')), may hold values from -1 to 1
- correlation_root: float32 [16384, 1536], P('rows'), may hold values from -1 to 2
- pattern: int32 [512, 48], replicated, may hold values from 0 to 1
- sub_blocks: int32 [512, 16], P(('rows', 'cols', 'space')), may hold values from 0 to 47, as said below
- sub_count: int32 [512], P(('rows', 'cols', 'space')), may hold values from 8 to 16, as said below
Outputs:
- density: float32 [16384, 1536], P(('rows', 'cols', 'space'))
- charges: float32 [16384], P(('rows', 'cols', 'space'))
The draws below stay inside these ranges and needn't reach their ends.
Inputs may be any that keep to these rules, and one draw needn't show every extreme that they name: `sub_blocks`: row g lists distinct positions; its first entry is 16 + g mod 16, the position of block g itself. `sub_count`: some submatrix has exactly 16 live blocks.
All inputs are finite; a program needn't handle non-finite values.
Results may differ from the reference program's by a relative error of at most 0.0003.
Values sent between devices are 32-bit elements; how exact they have to be, the bound alone decides.
No kernel may reach another device: no remote copies, remote signals or barrier semaphores. Data moves between devices by JAX's collectives and lax.ppermute only.
A program may use at most 128 MiB of HBM per device.

```python
import math
import jax
import jax.numpy as jnp
from jax import lax

BLK = 32
MAXB = 16
NPG = 16
SLAB = 512
WIN = 1536
WB = 48
NB = 512
N = 16384
N_ROWS = 32


def draw_hamiltonian(key, part):
    values = jnp.clip(jax.random.normal(key, (N, WIN), jnp.float32), -6.0, 6.0)
    return values / math.sqrt(WIN)


def draw_correlation_root(key, part):
    entries = jnp.clip(jax.random.normal(key, (N, WIN), jnp.float32), -6.0, 6.0)
    entries = entries * (0.6 / math.sqrt(WIN))
    row_ids = jnp.arange(N, dtype=jnp.int32)
    column_ids = jnp.arange(WIN, dtype=jnp.int32)
    diagonal = (column_ids[None, :] == SLAB + (row_ids % SLAB)[:, None]).astype(jnp.float32)
    return entries + diagonal


def draw_pattern(key, part):
    picks = jax.random.randint(key, (NB, WB), 0, 5)
    block_ids = jnp.arange(NB, dtype=jnp.int32)
    band_ids = jnp.arange(WB, dtype=jnp.int32)
    diagonal = band_ids[None, :] == NPG + (block_ids % NPG)[:, None]
    return jnp.where(diagonal | (picks < 3), 1, 0).astype(jnp.int32)


def draw_sub_blocks(key, part):
    key_list = jax.random.split(jax.random.fold_in(key, 11), NB)
    shuffled = jax.vmap(lambda single: jax.random.permutation(single, WB - 1))(key_list).astype(jnp.int32)
    home_slot = (NPG + jnp.arange(NB, dtype=jnp.int32) % NPG)[:, None]
    neighbours = shuffled + (shuffled >= home_slot).astype(jnp.int32)
    return jnp.concatenate([home_slot, neighbours[:, :MAXB - 1]], axis=1).astype(jnp.int32)


def draw_sub_count(key, part):
    block_counts = jax.random.randint(jax.random.fold_in(key, 5), (NB,), MAXB // 2, MAXB + 1)
    chosen_block = jax.random.randint(jax.random.fold_in(key, 6), (), 0, NB)
    return jnp.where(jnp.arange(NB, dtype=jnp.int32) == chosen_block, MAXB, block_counts).astype(jnp.int32)


def setup_inputs(seed: int = 0) -> dict:
    arg_keys = jax.random.split(jax.random.key(seed), 6)
    hamiltonian = draw_hamiltonian(jax.random.fold_in(arg_keys[5], 71), 0)
    correlation_root = draw_correlation_root(jax.random.fold_in(arg_keys[5], 71), 0)
    pattern = draw_pattern(jax.random.fold_in(arg_keys[5], 71), 0)
    sub_blocks = draw_sub_blocks(jax.random.fold_in(arg_keys[5], 71), 0)
    sub_count = draw_sub_count(jax.random.fold_in(arg_keys[5], 71), 0)
    return dict(hamiltonian=hamiltonian, correlation_root=correlation_root, pattern=pattern, sub_blocks=sub_blocks, sub_count=sub_count)


highest = lax.Precision.HIGHEST

def multiply(leftside, rightside):
    return jnp.dot(leftside, rightside, precision=highest, preferred_element_type=jnp.float32)

def windows(banded):
    stacked = banded.reshape(N_ROWS, SLAB, WIN)
    above_used = jnp.roll(stacked, 1, axis=0)[:, :, SLAB:]
    below_used = jnp.roll(stacked, -1, axis=0)[:, :, :2 * SLAB]
    zero_block = jnp.zeros((N_ROWS, SLAB, SLAB), jnp.float32)
    top_rows = jnp.concatenate([above_used, zero_block], axis=2)
    bottom = jnp.concatenate([zero_block, below_used], axis=2)
    return jnp.concatenate([top_rows, stacked, bottom], axis=1)

def sandwich_step(leftside, rightside, pattern_mask):
    stacked = leftside.reshape(N_ROWS, SLAB, WIN)
    joined = jnp.einsum('sik,skj->sij', stacked, windows(rightside), precision=highest)
    return pattern_mask * joined.reshape(N, WIN)

def density_rows(local_window, positions, live_count):
    offsets = (positions[:, None] * BLK + jnp.arange(BLK, dtype=jnp.int32)[None, :]).reshape(-1)
    live_cols = jnp.repeat((jnp.arange(MAXB, dtype=jnp.int32) < live_count).astype(jnp.float32), BLK)
    assembled = jnp.take(jnp.take(local_window, offsets, axis=0), offsets, axis=1)
    assembled = assembled * live_cols[:, None] * live_cols[None, :]
    symmetric = 0.5 * (assembled + assembled.T)
    live_order = (live_count * BLK).astype(jnp.float32)
    normalizer = jnp.sqrt(live_order) / (2.0 * jnp.sqrt(jnp.sum(symmetric * symmetric) + 1e-06))
    iterate = symmetric * normalizer
    square = multiply(iterate, iterate)
    iterate = 1.5 * iterate - 0.5 * multiply(iterate, square)
    square = multiply(iterate, iterate)
    home_rows = iterate[:BLK]
    home_rows = 1.5 * home_rows - 0.5 * multiply(home_rows, square)
    padded_order = MAXB * BLK
    home_eye = (jnp.arange(BLK, dtype=jnp.int32)[:, None] == jnp.arange(padded_order, dtype=jnp.int32)[None, :]).astype(jnp.float32)
    home_density = 0.5 * (home_eye - home_rows)
    placement = (offsets[:, None] == jnp.arange(local_window.shape[1], dtype=jnp.int32)[None, :]).astype(jnp.float32)
    return multiply(home_density, placement)

def reference(hamiltonian, correlation_root, pattern, sub_blocks, sub_count):
    pattern_mask = jnp.repeat(jnp.repeat(pattern.astype(jnp.float32), BLK, axis=0), BLK, axis=1)
    half_done = sandwich_step(hamiltonian, correlation_root, pattern_mask)
    orthogonal = sandwich_step(correlation_root, half_done, pattern_mask)
    ortho_windows = windows(orthogonal)

    def solve_block(entries):
        block_index, positions, live_count = entries
        slab_index = (block_index // NPG).astype(jnp.int32)
        local_window = lax.dynamic_index_in_dim(ortho_windows, slab_index, 0, keepdims=False)
        return density_rows(local_window, positions, live_count)
    density_blocks = lax.map(solve_block, (jnp.arange(NB, dtype=jnp.int32), sub_blocks, sub_count))
    density_band = density_blocks.reshape(N, WIN)
    half_back = sandwich_step(density_band, correlation_root, pattern_mask)
    density = sandwich_step(correlation_root, half_back, pattern_mask)
    charges = lax.optimization_barrier(jnp.sum(density, axis=1))
    return (density, charges)
```

```python
import functools

import jax
import jax.numpy as jnp
from jax import lax
from jax.experimental import pallas as pl
from jax.experimental.pallas import tpu as pltpu
from jax.sharding import PartitionSpec as P

BLK = 32
MAXB = 16
SLAB = 512
CHUNK = 64
LANES = 256
ORDER = MAXB * BLK
PIECES = 7 * CHUNK
f32 = jnp.float32
bf16 = jnp.bfloat16
ALL = ("cols", "space")
VMEM = pl.BlockSpec(memory_space=pltpu.VMEM)
SMEM = pl.BlockSpec(memory_space=pltpu.SMEM)
PARAMS = pltpu.CompilerParams(vmem_limit_bytes=56 * 1024 * 1024)


def passed_along(value, axis, steps):
    count = lax.axis_size(axis)
    pairs = [(source, (source + steps) % count) for source in range(count)]
    return lax.ppermute(value, axis, pairs)


def kernel_call(body, shapes, operands, in_specs, scratch=(), flops=0, moved=0):
    return pl.pallas_call(
        body,
        out_shape=shapes,
        in_specs=in_specs,
        out_specs=jax.tree.map(lambda _: VMEM, shapes),
        scratch_shapes=list(scratch),
        compiler_params=PARAMS,
        cost_estimate=pl.CostEstimate(flops=flops, bytes_accessed=moved, transcendentals=0),
    )(*operands)


def split(x):
    high = x.astype(bf16)
    return high, (x - high.astype(f32)).astype(bf16)


def dot3(a, b):
    dot = functools.partial(jnp.dot, preferred_element_type=f32)
    return dot(a[0], b[0]) + (dot(a[0], b[1]) + dot(a[1], b[0]))


def send_parts(full, own, up, down):
    own[...] = full
    up[...] = pltpu.roll(full, LANES - CHUNK, 1)[:, : 2 * CHUNK]
    down[...] = full[:, : 2 * CHUNK]


def window_parts(above, own, below):
    blank = jnp.zeros((SLAB, 2 * CHUNK), f32)
    return (
        jnp.concatenate([above, blank], axis=1),
        own,
        pltpu.roll(jnp.concatenate([below, blank], axis=1), CHUNK, 1),
    )


def split_kernel(root, above, own, below, root_hi, root_lo, win_hi, win_lo):
    root_hi[...], root_lo[...] = split(root[...])
    for k, part in enumerate(window_parts(above[...], own[...], below[...])):
        rows = slice(k * SLAB, (k + 1) * SLAB)
        win_hi[rows, :], win_lo[rows, :] = split(part)


def first_kernel(ham, win_hi, win_lo, mask, own, up, down):
    total = jnp.zeros((SLAB, LANES), f32)
    for k in range(3):
        cut = slice(k * SLAB, (k + 1) * SLAB)
        total += dot3(split(ham[:, cut]), (win_hi[cut, :], win_lo[cut, :]))
    send_parts(total * mask[...], own, up, down)


def root_product(root_hi, root_lo, above, own, below, mask):
    total = jnp.zeros((SLAB, LANES), f32)
    for k, part in enumerate(window_parts(above[...], own[...], below[...])):
        cut = slice(k * SLAB, (k + 1) * SLAB)
        total += dot3((root_hi[:, cut], root_lo[:, cut]), split(part))
    return total * mask[...]


def ortho_kernel(root_hi, root_lo, above, own, below, mask, mine, up, down):
    turned = root_product(root_hi, root_lo, above, own, below, mask).T
    mine[...] = turned[: 3 * CHUNK]
    up[...] = turned[CHUNK : 3 * CHUNK]
    down[...] = turned[: 2 * CHUNK]


def density_kernel(root_hi, root_lo, above, own, below, mask, packed):
    full = root_product(root_hi, root_lo, above, own, below, mask)
    half = CHUNK // 2
    for c in range(SLAB // CHUNK):
        rows = full[c * CHUNK : (c + 1) * CHUNK]
        packed[c, :CHUNK, :] = rows[:, : 2 * CHUNK]
        last = rows[:, 2 * CHUNK :]
        lane = lax.broadcasted_iota(jnp.int32, (half, 2 * CHUNK), 1)
        packed[c, CHUNK:, :] = jnp.where(lane < CHUNK, last[:half], pltpu.roll(last[half:], CHUNK, 1))


def solve_kernel(blocks, counts, gathered, out, assembled):
    lane_block = lax.broadcasted_iota(jnp.int32, (BLK, 128), 1) // BLK
    row_id = lax.broadcasted_iota(jnp.int32, (BLK, ORDER), 0)
    col_id = lax.broadcasted_iota(jnp.int32, (BLK, ORDER), 1)
    for g in range(2):
        live = counts[g]
        spots = []
        for i in range(MAXB):
            p = blocks[g, i]
            panel = p // 16
            tile = pl.multiple_of(((p % 16) // 4) * 128, 128)
            shift = lax.rem((i % 4 - p % 4) * BLK + 128, 128)
            spots.append((panel, tile, shift, i < live))

        def gather_row(k, carry):
            q = blocks[g, k]
            j = q // 16
            base = ((q % 16) // 2) * PIECES + (q % 2) * BLK + j * CHUNK
            starts = (base + 3 * CHUNK, base, base + 4 * CHUNK)
            row_live = k < live
            for t in range(4):
                total = jnp.zeros((BLK, 128), f32)
                for ii in range(4):
                    panel, tile, shift, col_live = spots[t * 4 + ii]
                    start = jnp.where(panel == 0, starts[0], jnp.where(panel == 1, starts[1], starts[2]))
                    start = pl.multiple_of(start, BLK)
                    here = row_live & col_live & (jnp.abs(panel - j) <= 1)
                    block = pltpu.roll(gathered[pl.ds(start, BLK), pl.ds(tile, 128)], shift, 1)
                    total = jnp.where(lane_block == jnp.where(here, ii, 9), block, total)
                assembled[pl.ds(pl.multiple_of(k * BLK, BLK), BLK), t * 128 : (t + 1) * 128] = total
            return carry

        lax.fori_loop(0, MAXB, gather_row, 0)
        whole = assembled[...]
        symmetric = 0.5 * (whole + whole.T)
        squares = jnp.sum(symmetric * symmetric, keepdims=True) + 1e-06
        size = jnp.full((1, 1), live * BLK, jnp.int32).astype(f32)
        iterate = symmetric * (jnp.sqrt(size) / (2.0 * jnp.sqrt(squares)))
        parts = split(iterate)
        square = split(dot3(parts, parts))
        iterate = 1.5 * iterate - 0.5 * dot3(parts, square)
        parts = split(iterate)
        home = iterate[:BLK]
        once = dot3((parts[0][:BLK], parts[1][:BLK]), parts)
        home = 1.5 * home - 0.5 * dot3(split(once), parts)
        out[g * BLK : (g + 1) * BLK, :] = 0.5 * (jnp.where(row_id == col_id, 1.0, 0.0) - home)


def back_kernel(blocks, places, rows, win_hi, win_lo, mask, own, up, down, full, part_hi, part_lo):
    def one_block(e, carry):
        g = places[e]
        for i in range(MAXB):
            source = pl.ds(pl.multiple_of(blocks[g, i] * BLK, BLK), BLK)
            target = slice(i * BLK, (i + 1) * BLK)
            part_hi[target, :] = win_hi[source, :]
            part_lo[target, :] = win_lo[source, :]
        home = split(rows[pl.ds(pl.multiple_of(e * BLK, BLK), BLK), :])
        there = pl.ds(pl.multiple_of(g * BLK, BLK), BLK)
        full[there, :] = dot3(home, (part_hi[...], part_lo[...])) * mask[there, :]
        return carry

    lax.fori_loop(0, SLAB // BLK, one_block, 0)
    send_parts(full[...], own, up, down)


def final_kernel(packed, density, charges):
    half = CHUNK // 2
    first = lax.broadcasted_iota(jnp.int32, (CHUNK, 128), 1) < CHUNK
    total = jnp.zeros((CHUNK, 128), f32)
    for m in range(SLAB // (2 * CHUNK)):
        a, b = packed[2 * m], packed[2 * m + 1]
        ab, bb = a[:CHUNK], b[:CHUNK]
        a2, b2 = a[CHUNK:], b[CHUNK:]
        left = jnp.where(first, ab, pltpu.roll(bb, CHUNK, 1))
        middle = jnp.where(first, pltpu.roll(ab, CHUNK, 1), bb)
        right = jnp.concatenate(
            [
                jnp.where(first[:half], a2, pltpu.roll(b2, CHUNK, 1)),
                jnp.where(first[:half], pltpu.roll(a2, CHUNK, 1), b2),
            ],
            axis=0,
        )
        for j, part in enumerate((left, middle, right)):
            density[:, j * SLAB + m * 128 : j * SLAB + (m + 1) * 128] = part
        total += left + middle + right
    charges[...] = jnp.sum(total, axis=1, keepdims=True)


def shards(hamiltonian, root, pattern, sub_blocks, sub_count):
    sds = jax.ShapeDtypeStruct
    slab = lax.axis_index("rows")
    col, core = lax.axis_index("cols"), lax.axis_index("space")
    home = 2 * col + core
    parts = (sds((SLAB, LANES), f32), sds((SLAB, 2 * CHUNK), f32), sds((SLAB, 2 * CHUNK), f32))
    product = dict(flops=6 * SLAB * 3 * SLAB * LANES, moved=6 << 20)

    with jax.named_scope("inputs"):
        ham = lax.all_gather(hamiltonian, ALL, axis=0, tiled=True)
        pieces = [lax.dynamic_slice(root, (0, j * SLAB + home * CHUNK), (SLAB, CHUNK)) for j in range(3)]
        above = passed_along(jnp.concatenate(pieces[1:], axis=1), "rows", 1)
        below = passed_along(jnp.concatenate(pieces[:2], axis=1), "rows", -1)
        own = jnp.concatenate(pieces + [jnp.zeros((SLAB, CHUNK), f32)], axis=1)
        mask = lax.dynamic_slice(pattern, (slab * 16, 0), (16, 48)).astype(f32).reshape(16, 3, 16)
        mask = lax.dynamic_slice(mask, (0, 0, 2 * home), (16, 3, 2)).reshape(16, 6)
        mask = jnp.pad(mask, ((0, 0), (0, 2)))
        mask = jnp.broadcast_to(mask[:, None, :, None], (16, BLK, 8, BLK)).reshape(SLAB, LANES)
        root_hi, root_lo, win_hi, win_lo = kernel_call(
            split_kernel,
            (sds((SLAB, 3 * SLAB), bf16),) * 2 + (sds((3 * SLAB, LANES), bf16),) * 2,
            (root, above, own, below),
            [VMEM] * 4,
            flops=1 << 22,
            moved=8 << 20,
        )
    with jax.named_scope("half_done"):
        own, up, down = kernel_call(
            first_kernel, parts, (ham, win_hi, win_lo, mask), [VMEM] * 4, **product
        )
        above, below = passed_along(up, "rows", 1), passed_along(down, "rows", -1)
    with jax.named_scope("orthogonal"):
        mine, up, down = kernel_call(
            ortho_kernel,
            (sds((3 * CHUNK, SLAB), f32), sds((2 * CHUNK, SLAB), f32), sds((2 * CHUNK, SLAB), f32)),
            (root_hi, root_lo, above, own, below, mask),
            [VMEM] * 6,
            **product,
        )
        above, below = passed_along(up, "rows", 1), passed_along(down, "rows", -1)
        gathered = lax.all_gather(jnp.concatenate([mine, above, below], axis=0), ALL, axis=0, tiled=True)
    with jax.named_scope("lists"):
        lists, _ = lax.optimization_barrier((sub_blocks, ham[:8, :128]))
        lists = lax.all_gather(lists, ALL, axis=0, tiled=True)
    with jax.named_scope("solve"):
        rows = kernel_call(
            solve_kernel,
            sds((2 * BLK, ORDER), f32),
            (sub_blocks, sub_count, gathered),
            [SMEM, SMEM, VMEM],
            scratch=[pltpu.VMEM((ORDER, ORDER), f32)],
            flops=12 * ORDER**3,
            moved=8 << 20,
        )
    with jax.named_scope("share"):
        near = [rows] + [passed_along(rows, "cols", steps) for steps in (1, -1, 2)]
        far = [passed_along(r, "space", 1) for r in near]
        shared = jnp.concatenate(near + far, axis=0)
        chips = jnp.stack([col, (col + 3) % 4, (col + 1) % 4, (col + 2) % 4])
        order = jnp.concatenate([2 * chips + core, 2 * chips + 1 - core])
        places = (2 * order[:, None] + jnp.arange(2)[None, :]).reshape(-1).astype(jnp.int32)
    with jax.named_scope("half_back"):
        own, up, down = kernel_call(
            back_kernel,
            parts,
            (lists, places, shared, win_hi, win_lo, mask),
            [SMEM, SMEM] + [VMEM] * 4,
            scratch=[
                pltpu.VMEM((SLAB, LANES), f32),
                pltpu.VMEM((ORDER, LANES), bf16),
                pltpu.VMEM((ORDER, LANES), bf16),
            ],
            **product,
        )
        above, below = passed_along(up, "rows", 1), passed_along(down, "rows", -1)
    with jax.named_scope("density"):
        packed = kernel_call(
            density_kernel,
            sds((SLAB // CHUNK, 3 * CHUNK // 2, 2 * CHUNK), f32),
            (root_hi, root_lo, above, own, below, mask),
            [VMEM] * 6,
            **product,
        )
        packed = lax.all_to_all(packed, ALL, 0, 0)
        density, charges = kernel_call(
            final_kernel,
            (sds((CHUNK, 3 * SLAB), f32), sds((CHUNK, 1), f32)),
            (packed,),
            [VMEM],
            flops=1 << 20,
            moved=1 << 20,
        )
    return density, charges.reshape(CHUNK)


def solution(mesh):
    return jax.shard_map(
        shards,
        mesh=mesh,
        in_specs=(
            P(("rows", "cols", "space"), None),
            P("rows", None),
            P(),
            P(("rows", "cols", "space"), None),
            P(("rows", "cols", "space")),
        ),
        out_specs=(P(("rows", "cols", "space"), None), P(("rows", "cols", "space"))),
        check_vma=False,
    )
```

```python
import functools

import jax
import jax.numpy as jnp
from jax import lax
from jax.experimental import pallas as pl
from jax.experimental.pallas import tpu as pltpu
from jax.sharding import PartitionSpec as P

BLK = 32
MAXB = 16
SLAB = 512
CHUNK = 64
LANES = 256
ORDER = MAXB * BLK
OWN_ROWS = 3 * SLAB
NEAR = 4 * CHUNK
f32 = jnp.float32
bf16 = jnp.bfloat16
ALL = ("cols", "space")
VMEM = pl.BlockSpec(memory_space=pltpu.VMEM)
SMEM = pl.BlockSpec(memory_space=pltpu.SMEM)
PARAMS = pltpu.CompilerParams(vmem_limit_bytes=56 * 1024 * 1024)


def passed_along(value, axis, steps):
    count = lax.axis_size(axis)
    pairs = [(source, (source + steps) % count) for source in range(count)]
    return lax.ppermute(value, axis, pairs)


def kernel_call(body, shapes, operands, in_specs, scratch=(), flops=0, moved=0):
    return pl.pallas_call(
        body,
        out_shape=shapes,
        in_specs=in_specs,
        out_specs=jax.tree.map(lambda _: VMEM, shapes),
        scratch_shapes=list(scratch),
        compiler_params=PARAMS,
        cost_estimate=pl.CostEstimate(flops=flops, bytes_accessed=moved, transcendentals=0),
    )(*operands)


def split(x):
    high = x.astype(bf16)
    return high, (x - high.astype(f32)).astype(bf16)


def dot3(a, b):
    dot = functools.partial(jnp.dot, preferred_element_type=f32)
    return dot(a[0], b[0]) + (dot(a[0], b[1]) + dot(a[1], b[0]))


def send_parts(full, own, up, down):
    own[...] = full
    up[...] = pltpu.roll(full, LANES - CHUNK, 1)[:, : 2 * CHUNK]
    down[...] = full[:, : 2 * CHUNK]


def window_parts(above, own, below):
    blank = jnp.zeros((SLAB, 2 * CHUNK), f32)
    return (
        jnp.concatenate([above, blank], axis=1),
        own,
        pltpu.roll(jnp.concatenate([below, blank], axis=1), CHUNK, 1),
    )


def split_kernel(root, above, own, below, root_hi, root_lo, win_hi, win_lo):
    root_hi[...], root_lo[...] = split(root[...])
    for k, part in enumerate(window_parts(above[...], own[...], below[...])):
        rows = slice(k * SLAB, (k + 1) * SLAB)
        win_hi[rows, :], win_lo[rows, :] = split(part)


def first_kernel(ham, win_hi, win_lo, mask, own, up, down):
    total = jnp.zeros((SLAB, LANES), f32)
    for k in range(3):
        cut = slice(k * SLAB, (k + 1) * SLAB)
        total += dot3(split(ham[:, cut]), (win_hi[cut, :], win_lo[cut, :]))
    send_parts(total * mask[...], own, up, down)


def root_product(root_hi, root_lo, above, own, below, mask):
    total = jnp.zeros((SLAB, LANES), f32)
    for k, part in enumerate(window_parts(above[...], own[...], below[...])):
        cut = slice(k * SLAB, (k + 1) * SLAB)
        total += dot3((root_hi[:, cut], root_lo[:, cut]), split(part))
    return total * mask[...]


def ortho_kernel(root_hi, root_lo, above, own, below, mask, mine, up, down):
    turned = root_product(root_hi, root_lo, above, own, below, mask).T
    mine[...] = turned[: 3 * CHUNK]
    up[...] = turned[CHUNK : 3 * CHUNK]
    down[...] = turned[: 2 * CHUNK]


def density_kernel(root_hi, root_lo, above, own, below, mask, packed):
    full = root_product(root_hi, root_lo, above, own, below, mask)
    half = CHUNK // 2
    for c in range(SLAB // CHUNK):
        rows = full[c * CHUNK : (c + 1) * CHUNK]
        packed[c, :CHUNK, :] = rows[:, : 2 * CHUNK]
        last = rows[:, 2 * CHUNK :]
        lane = lax.broadcasted_iota(jnp.int32, (half, 2 * CHUNK), 1)
        packed[c, CHUNK:, :] = jnp.where(lane < CHUNK, last[:half], pltpu.roll(last[half:], CHUNK, 1))


def solve_kernel(blocks, counts, slots, own, *rest):
    near, (out, gathered, assembled, sems) = rest[:-4], rest[-4:]
    copies = [pltpu.make_async_copy(own, gathered.at[pl.ds(0, OWN_ROWS)], sems.at[0])]
    at = OWN_ROWS
    for n, piece in enumerate(near):
        target = gathered.at[pl.ds(at, piece.shape[0])]
        copies.append(pltpu.make_async_copy(piece, target, sems.at[n + 1]))
        at += piece.shape[0]
    for copy in copies:
        copy.start()
    for copy in copies:
        copy.wait()
    lane_block = lax.broadcasted_iota(jnp.int32, (BLK, 128), 1) // BLK
    row_id = lax.broadcasted_iota(jnp.int32, (BLK, ORDER), 0)
    col_id = lax.broadcasted_iota(jnp.int32, (BLK, ORDER), 1)
    for g in range(2):
        live = counts[g]
        spots = []
        for i in range(MAXB):
            p = blocks[g, i]
            panel = p // 16
            tile = pl.multiple_of(((p % 16) // 4) * 128, 128)
            shift = lax.rem((i % 4 - p % 4) * BLK + 128, 128)
            spots.append((panel, tile, shift, i < live))

        def gather_row(k, carry):
            q = blocks[g, k]
            j = q // 16
            c = (q % 16) // 2
            base = (q % 2) * BLK + j * CHUNK
            away = OWN_ROWS + slots[c] * NEAR + base
            starts = (away, c * 3 * CHUNK + base, away + CHUNK)
            row_live = k < live
            for t in range(4):
                total = jnp.zeros((BLK, 128), f32)
                for ii in range(4):
                    panel, tile, shift, col_live = spots[t * 4 + ii]
                    start = jnp.where(panel == 0, starts[0], jnp.where(panel == 1, starts[1], starts[2]))
                    start = pl.multiple_of(start, BLK)
                    here = row_live & col_live & (jnp.abs(panel - j) <= 1)
                    block = pltpu.roll(gathered[pl.ds(start, BLK), pl.ds(tile, 128)], shift, 1)
                    total = jnp.where(lane_block == jnp.where(here, ii, 9), block, total)
                assembled[pl.ds(pl.multiple_of(k * BLK, BLK), BLK), t * 128 : (t + 1) * 128] = total
            return carry

        lax.fori_loop(0, MAXB, gather_row, 0)
        whole = assembled[...]
        symmetric = 0.5 * (whole + whole.T)
        squares = jnp.sum(symmetric * symmetric, keepdims=True) + 1e-06
        size = jnp.full((1, 1), live * BLK, jnp.int32).astype(f32)
        iterate = symmetric * (jnp.sqrt(size) / (2.0 * jnp.sqrt(squares)))
        parts = split(iterate)
        square = split(dot3(parts, parts))
        iterate = 1.5 * iterate - 0.5 * dot3(parts, square)
        parts = split(iterate)
        home = iterate[:BLK]
        once = dot3((parts[0][:BLK], parts[1][:BLK]), parts)
        home = 1.5 * home - 0.5 * dot3(split(once), parts)
        out[g * BLK : (g + 1) * BLK, :] = 0.5 * (jnp.where(row_id == col_id, 1.0, 0.0) - home)


def back_kernel(blocks, places, rows, win_hi, win_lo, mask, own, up, down, full, part_hi, part_lo):
    def one_block(e, carry):
        g = places[e]
        for i in range(MAXB):
            source = pl.ds(pl.multiple_of(blocks[g, i] * BLK, BLK), BLK)
            target = slice(i * BLK, (i + 1) * BLK)
            part_hi[target, :] = win_hi[source, :]
            part_lo[target, :] = win_lo[source, :]
        home = split(rows[pl.ds(pl.multiple_of(e * BLK, BLK), BLK), :])
        there = pl.ds(pl.multiple_of(g * BLK, BLK), BLK)
        full[there, :] = dot3(home, (part_hi[...], part_lo[...])) * mask[there, :]
        return carry

    lax.fori_loop(0, SLAB // BLK, one_block, 0)
    send_parts(full[...], own, up, down)


def final_kernel(packed, density, charges):
    half = CHUNK // 2
    first = lax.broadcasted_iota(jnp.int32, (CHUNK, 128), 1) < CHUNK
    total = jnp.zeros((CHUNK, 128), f32)
    for m in range(SLAB // (2 * CHUNK)):
        a, b = packed[2 * m], packed[2 * m + 1]
        ab, bb = a[:CHUNK], b[:CHUNK]
        a2, b2 = a[CHUNK:], b[CHUNK:]
        left = jnp.where(first, ab, pltpu.roll(bb, CHUNK, 1))
        middle = jnp.where(first, pltpu.roll(ab, CHUNK, 1), bb)
        right = jnp.concatenate(
            [
                jnp.where(first[:half], a2, pltpu.roll(b2, CHUNK, 1)),
                jnp.where(first[:half], pltpu.roll(a2, CHUNK, 1), b2),
            ],
            axis=0,
        )
        for j, part in enumerate((left, middle, right)):
            density[:, j * SLAB + m * 128 : j * SLAB + (m + 1) * 128] = part
        total += left + middle + right
    charges[...] = jnp.sum(total.T, axis=0, keepdims=True)


def shards(hamiltonian, root, pattern, sub_blocks, sub_count):
    sds = jax.ShapeDtypeStruct
    slab = lax.axis_index("rows")
    col, core = lax.axis_index("cols"), lax.axis_index("space")
    home = 2 * col + core
    parts = (sds((SLAB, LANES), f32), sds((SLAB, 2 * CHUNK), f32), sds((SLAB, 2 * CHUNK), f32))
    product = dict(flops=6 * SLAB * 3 * SLAB * LANES, moved=6 << 20)

    with jax.named_scope("inputs"):
        ham = lax.all_gather(hamiltonian, ALL, axis=0, tiled=True)
        pieces = [lax.dynamic_slice(root, (0, j * SLAB + home * CHUNK), (SLAB, CHUNK)) for j in range(3)]
        above = passed_along(jnp.concatenate(pieces[1:], axis=1), "rows", 1)
        below = passed_along(jnp.concatenate(pieces[:2], axis=1), "rows", -1)
        own = jnp.concatenate(pieces + [jnp.zeros((SLAB, CHUNK), f32)], axis=1)
        mask = lax.dynamic_slice(pattern, (slab * 16, 0), (16, 48)).astype(f32).reshape(16, 3, 16)
        mask = lax.dynamic_slice(mask, (0, 0, 2 * home), (16, 3, 2)).reshape(16, 6)
        mask = jnp.pad(mask, ((0, 0), (0, 2)))
        mask = jnp.broadcast_to(mask[:, None, :, None], (16, BLK, 8, BLK)).reshape(SLAB, LANES)
        root_hi, root_lo, win_hi, win_lo = kernel_call(
            split_kernel,
            (sds((SLAB, 3 * SLAB), bf16),) * 2 + (sds((3 * SLAB, LANES), bf16),) * 2,
            (root, above, own, below),
            [VMEM] * 4,
            flops=1 << 22,
            moved=8 << 20,
        )
        lists = lax.all_gather(sub_blocks, ALL, axis=0, tiled=True)
        win_hi, lists = lax.optimization_barrier((win_hi, lists))
    with jax.named_scope("half_done"):
        own, up, down = kernel_call(
            first_kernel, parts, (ham, win_hi, win_lo, mask), [VMEM] * 4, **product
        )
        above, below = passed_along(up, "rows", 1), passed_along(down, "rows", -1)
    with jax.named_scope("orthogonal"):
        mine, up, down = kernel_call(
            ortho_kernel,
            (sds((3 * CHUNK, SLAB), f32), sds((2 * CHUNK, SLAB), f32), sds((2 * CHUNK, SLAB), f32)),
            (root_hi, root_lo, above, own, below, mask),
            [VMEM] * 6,
            **product,
        )
        above, below = passed_along(up, "rows", 1), passed_along(down, "rows", -1)
        whole = lax.all_gather(mine, ALL, axis=0, tiled=True)
        near = jnp.concatenate([above, below], axis=0)
        before, after = passed_along(near, "cols", 1), passed_along(near, "cols", -1)
        half = NEAR // 2
        opposite = (passed_along(before[:half], "cols", 1), passed_along(after[half:], "cols", -1))
        near = (near, before, after) + opposite
        near = near + tuple(passed_along(piece, "space", 1) for piece in near)
        steps = jnp.arange(SLAB // CHUNK)
        turn = lax.rem(steps // 2 - col + 4, 4)
        slots = jnp.where(turn == 3, 1, jnp.where(turn == 0, 0, turn + 1))
        slots = (slots + 4 * lax.rem(steps + core, 2)).astype(jnp.int32)
    with jax.named_scope("solve"):
        rows = kernel_call(
            solve_kernel,
            sds((2 * BLK, ORDER), f32),
            (sub_blocks, sub_count, slots, whole) + near,
            [SMEM] * 3 + [pl.BlockSpec(memory_space=pl.ANY)] * 11,
            scratch=[
                pltpu.VMEM((OWN_ROWS + 8 * NEAR, SLAB), f32),
                pltpu.VMEM((ORDER, ORDER), f32),
                pltpu.SemaphoreType.DMA((11,)),
            ],
            flops=12 * ORDER**3,
            moved=8 << 20,
        )
    with jax.named_scope("share"):
        near = [rows] + [passed_along(rows, "cols", steps) for steps in (1, -1, 2)]
        far = [passed_along(r, "space", 1) for r in near]
        shared = jnp.concatenate(near + far, axis=0)
        chips = jnp.stack([col, (col + 3) % 4, (col + 1) % 4, (col + 2) % 4])
        order = jnp.concatenate([2 * chips + core, 2 * chips + 1 - core])
        places = (2 * order[:, None] + jnp.arange(2)[None, :]).reshape(-1).astype(jnp.int32)
    with jax.named_scope("half_back"):
        own, up, down = kernel_call(
            back_kernel,
            parts,
            (lists, places, shared, win_hi, win_lo, mask),
            [SMEM, SMEM] + [VMEM] * 4,
            scratch=[
                pltpu.VMEM((SLAB, LANES), f32),
                pltpu.VMEM((ORDER, LANES), bf16),
                pltpu.VMEM((ORDER, LANES), bf16),
            ],
            **product,
        )
        above, below = passed_along(up, "rows", 1), passed_along(down, "rows", -1)
    with jax.named_scope("density"):
        packed = kernel_call(
            density_kernel,
            sds((SLAB // CHUNK, 3 * CHUNK // 2, 2 * CHUNK), f32),
            (root_hi, root_lo, above, own, below, mask),
            [VMEM] * 6,
            **product,
        )
        packed = lax.all_to_all(packed, ALL, 0, 0)
        density, charges = kernel_call(
            final_kernel,
            (sds((CHUNK, 3 * SLAB), f32), sds((1, CHUNK), f32)),
            (packed,),
            [VMEM],
            flops=1 << 20,
            moved=1 << 20,
        )
    return density, charges.reshape(CHUNK)


def solution(mesh):
    return jax.shard_map(
        shards,
        mesh=mesh,
        in_specs=(
            P(("rows", "cols", "space"), None),
            P("rows", None),
            P(),
            P(("rows", "cols", "space"), None),
            P(("rows", "cols", "space")),
        ),
        out_specs=(P(("rows", "cols", "space"), None), P(("rows", "cols", "space"))),
        check_vma=False,
    )
```

```python
import functools

import jax
import jax.numpy as jnp
from jax import lax
from jax.experimental import pallas as pl
from jax.experimental.pallas import tpu as pltpu
from jax.sharding import PartitionSpec as P

BLK = 32
MAXB = 16
SLAB = 512
CHUNK = 64
LANES = 256
ORDER = MAXB * BLK
NEAR = 4 * CHUNK
f32 = jnp.float32
bf16 = jnp.bfloat16
ALL = ("cols", "space")
VMEM = pl.BlockSpec(memory_space=pltpu.VMEM)
SMEM = pl.BlockSpec(memory_space=pltpu.SMEM)


def passed_along(value, axis, steps):
    count = lax.axis_size(axis)
    pairs = [(source, (source + steps) % count) for source in range(count)]
    return lax.ppermute(value, axis, pairs)


def kernel_call(body, shapes, operands, in_specs, scratch=(), limit=12, flops=0, moved=0):
    return pl.pallas_call(
        body,
        out_shape=shapes,
        in_specs=in_specs,
        out_specs=jax.tree.map(lambda _: VMEM, shapes),
        scratch_shapes=list(scratch),
        compiler_params=pltpu.CompilerParams(vmem_limit_bytes=limit << 20),
        cost_estimate=pl.CostEstimate(flops=flops, bytes_accessed=moved, transcendentals=0),
    )(*operands)


def split(x):
    high = x.astype(bf16)
    return high, (x - high.astype(f32)).astype(bf16)


def dot3(a, b):
    dot = functools.partial(jnp.dot, preferred_element_type=f32)
    return dot(a[0], b[0]) + (dot(a[0], b[1]) + dot(a[1], b[0]))


def send_parts(full, own, up, down):
    own[...] = full
    up[...] = pltpu.roll(full, LANES - CHUNK, 1)[:, : 2 * CHUNK]
    down[...] = full[:, : 2 * CHUNK]


def window_parts(above, own, below):
    blank = jnp.zeros((SLAB, 2 * CHUNK), f32)
    return (
        jnp.concatenate([above, blank], axis=1),
        own,
        pltpu.roll(jnp.concatenate([below, blank], axis=1), CHUNK, 1),
    )


def split_kernel(root, above, own, below, root_hi, root_lo, win_hi, win_lo):
    root_hi[...], root_lo[...] = split(root[...])
    for k, part in enumerate(window_parts(above[...], own[...], below[...])):
        rows = slice(k * SLAB, (k + 1) * SLAB)
        win_hi[rows, :], win_lo[rows, :] = split(part)


def first_kernel(ham, win_hi, win_lo, mask, own, up, down):
    total = jnp.zeros((SLAB, LANES), f32)
    for k in range(3):
        cut = slice(k * SLAB, (k + 1) * SLAB)
        total += dot3(split(ham[:, cut]), (win_hi[cut, :], win_lo[cut, :]))
    send_parts(total * mask[...], own, up, down)


def root_product(root_hi, root_lo, above, own, below, mask):
    total = jnp.zeros((SLAB, LANES), f32)
    for k, part in enumerate(window_parts(above[...], own[...], below[...])):
        cut = slice(k * SLAB, (k + 1) * SLAB)
        total += dot3((root_hi[:, cut], root_lo[:, cut]), split(part))
    return total * mask[...]


def ortho_kernel(root_hi, root_lo, above, own, below, mask, mine, up, down):
    turned = root_product(root_hi, root_lo, above, own, below, mask).T
    mine[...] = turned[: 3 * CHUNK]
    up[...] = turned[CHUNK : 3 * CHUNK]
    down[...] = turned[: 2 * CHUNK]


def density_kernel(root_hi, root_lo, above, own, below, mask, packed):
    full = root_product(root_hi, root_lo, above, own, below, mask)
    half = CHUNK // 2
    for c in range(SLAB // CHUNK):
        rows = full[c * CHUNK : (c + 1) * CHUNK]
        packed[c, :CHUNK, :] = rows[:, : 2 * CHUNK]
        last = rows[:, 2 * CHUNK :]
        lane = lax.broadcasted_iota(jnp.int32, (half, 2 * CHUNK), 1)
        packed[c, CHUNK:, :] = jnp.where(lane < CHUNK, last[:half], pltpu.roll(last[half:], CHUNK, 1))


def solve_kernel(blocks, counts, slots, whole, near, out, rows, turned, assembled):
    row_id = lax.broadcasted_iota(jnp.int32, (BLK, ORDER), 0)
    col_id = lax.broadcasted_iota(jnp.int32, (BLK, ORDER), 1)
    dot = functools.partial(jnp.dot, preferred_element_type=f32)

    def gather(g):
        def one_row(k, carry):
            q = blocks[g, k]
            j, c = q // 16, (q % 16) // 2
            base = (q % 2) * BLK + j * CHUNK
            away = slots[c] * NEAR + base
            there = pl.ds(pl.multiple_of(k * BLK, BLK), BLK)
            sources = ((near, away), (whole, c * 3 * CHUNK + base), (near, away + CHUNK))
            for panel, (source, start) in enumerate(sources):
                keep = (k < counts[g]) & (jnp.abs(j - panel) <= 1)
                block = source[pl.ds(pl.multiple_of(start, BLK), BLK), :]
                rows[there, panel * SLAB : (panel + 1) * SLAB] = jnp.where(keep, block, 0.0)
            return carry

        def one_column(k, carry):
            source = pl.ds(pl.multiple_of(blocks[g, k] * BLK, BLK), BLK)
            there = pl.ds(pl.multiple_of(k * BLK, BLK), BLK)
            assembled[g, there, :] = jnp.where(k < counts[g], turned[source, :], 0.0)
            return carry

        lax.fori_loop(0, MAXB, one_row, 0, unroll=4)
        for panel in range(3):
            cut = slice(panel * SLAB, (panel + 1) * SLAB)
            turned[cut, :] = rows[:, cut].T
        lax.fori_loop(0, MAXB, one_column, 0, unroll=4)

    def scaled(g):
        whole_block = assembled[g]
        symmetric = 0.5 * (whole_block + whole_block.T)
        squares = jnp.sum(symmetric * symmetric, keepdims=True) + 1e-06
        size = jnp.full((1, 1), counts[g] * BLK, jnp.int32).astype(f32)
        return symmetric * (jnp.sqrt(size) / (2.0 * jnp.sqrt(squares)))

    def step(iterate):
        parts = split(iterate)
        return 1.5 * iterate - 0.5 * dot3(parts, split(dot3(parts, parts)))

    def thin(home, parts):
        high, low = split(home)
        both = dot(jnp.concatenate([high, low], axis=0), parts[0])
        return both[:BLK] + both[BLK:] + dot(high, parts[1])

    for g in range(2):
        gather(g)
    iterates = [step(iterate) for iterate in [scaled(g) for g in range(2)]]
    for g, iterate in enumerate(iterates):
        parts = split(iterate)
        home = iterate[:BLK]
        home = 1.5 * home - 0.5 * thin(thin(home, parts), parts)
        out[g * BLK : (g + 1) * BLK, :] = 0.5 * (jnp.where(row_id == col_id, 1.0, 0.0) - home)


def back_kernel(blocks, places, rows, win_hi, win_lo, mask, own, up, down, full, part_hi, part_lo):
    dot = functools.partial(jnp.dot, preferred_element_type=f32)
    width = part_hi.shape[0]

    def some_blocks(step, carry):
        for slot in range(width):
            e = step * width + slot
            g = places[e]
            for i in range(MAXB):
                source = pl.ds(pl.multiple_of(blocks[g, i] * BLK, BLK), BLK)
                target = slice(i * BLK, (i + 1) * BLK)
                part_hi[slot, target, :] = win_hi[source, :]
                part_lo[slot, target, :] = win_lo[source, :]
            high, low = split(rows[pl.ds(pl.multiple_of(e * BLK, BLK), BLK), :])
            both = dot(jnp.concatenate([high, low], axis=0), part_hi[slot])
            there = pl.ds(pl.multiple_of(g * BLK, BLK), BLK)
            total = both[:BLK] + both[BLK:] + dot(high, part_lo[slot])
            full[there, :] = total * mask[there, :]
        return carry

    lax.fori_loop(0, SLAB // BLK // width, some_blocks, 0)
    send_parts(full[...], own, up, down)


def final_kernel(packed, density, charges):
    half = CHUNK // 2
    first = lax.broadcasted_iota(jnp.int32, (CHUNK, 128), 1) < CHUNK
    total = jnp.zeros((CHUNK, 128), f32)
    for m in range(SLAB // (2 * CHUNK)):
        a, b = packed[2 * m], packed[2 * m + 1]
        ab, bb = a[:CHUNK], b[:CHUNK]
        a2, b2 = a[CHUNK:], b[CHUNK:]
        left = jnp.where(first, ab, pltpu.roll(bb, CHUNK, 1))
        middle = jnp.where(first, pltpu.roll(ab, CHUNK, 1), bb)
        right = jnp.concatenate(
            [
                jnp.where(first[:half], a2, pltpu.roll(b2, CHUNK, 1)),
                jnp.where(first[:half], pltpu.roll(a2, CHUNK, 1), b2),
            ],
            axis=0,
        )
        for j, part in enumerate((left, middle, right)):
            density[:, j * SLAB + m * 128 : j * SLAB + (m + 1) * 128] = part
        total += left + middle + right
    charges[...] = jnp.sum(total.T, axis=0, keepdims=True)


def shards(hamiltonian, root, pattern, sub_blocks, sub_count):
    sds = jax.ShapeDtypeStruct
    slab = lax.axis_index("rows")
    col, core = lax.axis_index("cols"), lax.axis_index("space")
    home = 2 * col + core
    parts = (sds((SLAB, LANES), f32), sds((SLAB, 2 * CHUNK), f32), sds((SLAB, 2 * CHUNK), f32))
    product = dict(flops=6 * SLAB * 3 * SLAB * LANES, moved=6 << 20)

    with jax.named_scope("inputs"):
        ham = lax.all_gather(hamiltonian, ALL, axis=0, tiled=True)
        pieces = [lax.dynamic_slice(root, (0, j * SLAB + home * CHUNK), (SLAB, CHUNK)) for j in range(3)]
        above = passed_along(jnp.concatenate(pieces[1:], axis=1), "rows", 1)
        below = passed_along(jnp.concatenate(pieces[:2], axis=1), "rows", -1)
        own = jnp.concatenate(pieces + [jnp.zeros((SLAB, CHUNK), f32)], axis=1)
        mask = lax.dynamic_slice(pattern, (slab * 16, 0), (16, 48)).astype(f32).reshape(16, 3, 16)
        mask = lax.dynamic_slice(mask, (0, 0, 2 * home), (16, 3, 2)).reshape(16, 6)
        mask = jnp.pad(mask, ((0, 0), (0, 2)))
        mask = jnp.broadcast_to(mask[:, None, :, None], (16, BLK, 8, BLK)).reshape(SLAB, LANES)
        root_hi, root_lo, win_hi, win_lo = kernel_call(
            split_kernel,
            (sds((SLAB, 3 * SLAB), bf16),) * 2 + (sds((3 * SLAB, LANES), bf16),) * 2,
            (root, above, own, below),
            [VMEM] * 4,
            flops=1 << 22,
            moved=8 << 20,
        )
        lists = lax.all_gather(sub_blocks, ALL, axis=0, tiled=True)
        win_hi, lists = lax.optimization_barrier((win_hi, lists))
    with jax.named_scope("half_done"):
        own, up, down = kernel_call(
            first_kernel, parts, (ham, win_hi, win_lo, mask), [VMEM] * 4, **product
        )
        above, below = passed_along(up, "rows", 1), passed_along(down, "rows", -1)
    with jax.named_scope("orthogonal"):
        mine, up, down = kernel_call(
            ortho_kernel,
            (sds((3 * CHUNK, SLAB), f32), sds((2 * CHUNK, SLAB), f32), sds((2 * CHUNK, SLAB), f32)),
            (root_hi, root_lo, above, own, below, mask),
            [VMEM] * 6,
            **product,
        )
        above, below = passed_along(up, "rows", 1), passed_along(down, "rows", -1)
        whole = lax.all_gather(mine, ALL, axis=0, tiled=True)
        near = jnp.concatenate([above, below], axis=0)
        before, after = passed_along(near, "cols", 1), passed_along(near, "cols", -1)
        half = NEAR // 2
        opposite = (passed_along(before[:half], "cols", 1), passed_along(after[half:], "cols", -1))
        near = (near, before, after) + opposite
        near = near + tuple(passed_along(piece, "space", 1) for piece in near)
        near = jnp.concatenate(near, axis=0)
        steps = jnp.arange(SLAB // CHUNK)
        turn = lax.rem(steps // 2 - col + 4, 4)
        slots = jnp.where(turn == 3, 1, jnp.where(turn == 0, 0, turn + 1))
        slots = (slots + 4 * lax.rem(steps + core, 2)).astype(jnp.int32)
    with jax.named_scope("solve"):
        rows = kernel_call(
            solve_kernel,
            sds((2 * BLK, ORDER), f32),
            (sub_blocks, sub_count, slots, whole, near),
            [SMEM] * 3 + [VMEM] * 2,
            scratch=[
                pltpu.VMEM((ORDER, 3 * SLAB), f32),
                pltpu.VMEM((3 * SLAB, ORDER), f32),
                pltpu.VMEM((2, ORDER, ORDER), f32),
            ],
            limit=24,
            flops=12 * ORDER**3,
            moved=8 << 20,
        )
    with jax.named_scope("share"):
        near = [rows] + [passed_along(rows, "cols", steps) for steps in (1, -1, 2)]
        far = [passed_along(r, "space", 1) for r in near]
        shared = jnp.concatenate(near + far, axis=0)
        chips = jnp.stack([col, (col + 3) % 4, (col + 1) % 4, (col + 2) % 4])
        order = jnp.concatenate([2 * chips + core, 2 * chips + 1 - core])
        places = (2 * order[:, None] + jnp.arange(2)[None, :]).reshape(-1).astype(jnp.int32)
    with jax.named_scope("half_back"):
        own, up, down = kernel_call(
            back_kernel,
            parts,
            (lists, places, shared, win_hi, win_lo, mask),
            [SMEM, SMEM] + [VMEM] * 4,
            scratch=[
                pltpu.VMEM((SLAB, LANES), f32),
                pltpu.VMEM((4, ORDER, LANES), bf16),
                pltpu.VMEM((4, ORDER, LANES), bf16),
            ],
            **product,
        )
        above, below = passed_along(up, "rows", 1), passed_along(down, "rows", -1)
    with jax.named_scope("density"):
        packed = kernel_call(
            density_kernel,
            sds((SLAB // CHUNK, 3 * CHUNK // 2, 2 * CHUNK), f32),
            (root_hi, root_lo, above, own, below, mask),
            [VMEM] * 6,
            **product,
        )
        packed = lax.all_to_all(packed, ALL, 0, 0)
        density, charges = kernel_call(
            final_kernel,
            (sds((CHUNK, 3 * SLAB), f32), sds((1, CHUNK), f32)),
            (packed,),
            [VMEM],
            flops=1 << 20,
            moved=1 << 20,
        )
    return density, charges.reshape(CHUNK)


def solution(mesh):
    return jax.shard_map(
        shards,
        mesh=mesh,
        in_specs=(
            P(("rows", "cols", "space"), None),
            P("rows", None),
            P(),
            P(("rows", "cols", "space"), None),
            P(("rows", "cols", "space")),
        ),
        out_specs=(P(("rows", "cols", "space"), None), P(("rows", "cols", "space"))),
        check_vma=False,
    )
```

```python
import functools

import jax
import jax.numpy as jnp
from jax import lax
from jax.experimental import pallas as pl
from jax.experimental.pallas import tpu as pltpu
from jax.sharding import PartitionSpec as P

BLK = 32
MAXB = 16
SLAB = 512
CHUNK = 64
LANES = 256
ORDER = MAXB * BLK
f32 = jnp.float32
bf16 = jnp.bfloat16
ALL = ("cols", "space")
VMEM = pl.BlockSpec(memory_space=pltpu.VMEM)
SMEM = pl.BlockSpec(memory_space=pltpu.SMEM)


def passed_along(value, axis, steps):
    count = lax.axis_size(axis)
    pairs = [(source, (source + steps) % count) for source in range(count)]
    return lax.ppermute(value, axis, pairs)


def around(value):
    return value, passed_along(value, "cols", 1), passed_along(value, "cols", -1)


def swapped(values):
    return values + tuple(passed_along(value, "space", 1) for value in values)


def shared(value):
    return swapped(around(value) + (passed_along(value, "cols", 2),))


def kernel_call(body, shapes, operands, in_specs, scratch=(), limit=12, flops=0, moved=0):
    return pl.pallas_call(
        body,
        out_shape=shapes,
        in_specs=in_specs,
        out_specs=jax.tree.map(lambda _: VMEM, shapes),
        scratch_shapes=list(scratch),
        compiler_params=pltpu.CompilerParams(vmem_limit_bytes=limit << 20),
        cost_estimate=pl.CostEstimate(flops=flops, bytes_accessed=moved, transcendentals=0),
    )(*operands)


def split(x):
    high = x.astype(bf16)
    return high, (x - high.astype(f32)).astype(bf16)


def dot3(a, b):
    dot = functools.partial(jnp.dot, preferred_element_type=f32)
    return dot(a[0], b[0]) + (dot(a[0], b[1]) + dot(a[1], b[0]))


def send_parts(full, own, up, down):
    own[...] = full
    up[...] = pltpu.roll(full, LANES - CHUNK, 1)[:, : 2 * CHUNK]
    down[...] = full[:, : 2 * CHUNK]


def window_parts(above, own, below):
    blank = jnp.zeros((SLAB, 2 * CHUNK), f32)
    return (
        jnp.concatenate([above, blank], axis=1),
        own,
        pltpu.roll(jnp.concatenate([below, blank], axis=1), CHUNK, 1),
    )


def split_kernel(root, above, own, below, root_hi, root_lo, win_hi, win_lo):
    root_hi[...], root_lo[...] = split(root[...])
    for k, part in enumerate(window_parts(above[...], own[...], below[...])):
        rows = slice(k * SLAB, (k + 1) * SLAB)
        win_hi[rows, :], win_lo[rows, :] = split(part)


def first_kernel(order, *refs):
    pieces, (win_hi, win_lo, mask, own, up, down, lists, ham_hi, ham_lo) = refs[:8], refs[8:]
    for n, piece in enumerate(pieces):
        there = pl.ds(pl.multiple_of(order[n] * CHUNK, CHUNK), CHUNK)
        ham_hi[there, :], ham_lo[there, :] = split(piece[:CHUNK, :])
        lists[2 * n : 2 * n + 2, :] = piece[CHUNK : CHUNK + 2, :128].astype(jnp.int32)
    total = jnp.zeros((SLAB, LANES), f32)
    for k in range(3):
        cut = slice(k * SLAB, (k + 1) * SLAB)
        total += dot3((ham_hi[:, cut], ham_lo[:, cut]), (win_hi[cut, :], win_lo[cut, :]))
    send_parts(total * mask[...], own, up, down)


def root_product(root_hi, root_lo, above, own, below, mask):
    total = jnp.zeros((SLAB, LANES), f32)
    for k, part in enumerate(window_parts(above[...], own[...], below[...])):
        cut = slice(k * SLAB, (k + 1) * SLAB)
        total += dot3((root_hi[:, cut], root_lo[:, cut]), split(part))
    return total * mask[...]


def ortho_kernel(root_hi, root_lo, above, own, below, mask, mine, up, down):
    turned = root_product(root_hi, root_lo, above, own, below, mask).T
    mine[...] = turned[: 3 * CHUNK]
    up[...] = turned[CHUNK : 3 * CHUNK]
    down[...] = turned[: 2 * CHUNK]


def density_kernel(root_hi, root_lo, above, own, below, mask, packed):
    full = root_product(root_hi, root_lo, above, own, below, mask)
    half = CHUNK // 2
    for c in range(SLAB // CHUNK):
        rows = full[c * CHUNK : (c + 1) * CHUNK]
        packed[c, :CHUNK, :] = rows[:, : 2 * CHUNK]
        last = rows[:, 2 * CHUNK :]
        lane = lax.broadcasted_iota(jnp.int32, (half, 2 * CHUNK), 1)
        packed[c, CHUNK:, :] = jnp.where(lane < CHUNK, last[:half], pltpu.roll(last[half:], CHUNK, 1))


def solve_kernel(blocks, counts, order, *refs):
    pieces, (out, inverse, rows, turned, assembled, valid) = refs[:24], refs[24:]
    row_id = lax.broadcasted_iota(jnp.int32, (BLK, ORDER), 0)
    col_id = lax.broadcasted_iota(jnp.int32, (BLK, ORDER), 1)
    list_id = lax.broadcasted_iota(jnp.int32, (1, ORDER), 1) // BLK
    dot = functools.partial(jnp.dot, preferred_element_type=f32)

    for g in range(2):
        for q in range(3 * 16):
            inverse[g, q] = MAXB
        for k in range(MAXB):
            inverse[g, blocks[g, k]] = k
    for n in range(8):
        for panel, piece, first in ((1, pieces[n], 0), (0, pieces[8 + n], 0), (2, pieces[16 + n], 1)):
            for at in range(piece.shape[0] // BLK):
                q = (first + at // 2) * 16 + 2 * order[n] + at % 2
                block = piece[at * BLK : (at + 1) * BLK, :]
                for g in range(2):
                    there = pl.ds(pl.multiple_of(inverse[g, q] * BLK, BLK), BLK)
                    rows[g, there, panel * SLAB : (panel + 1) * SLAB] = block

    def gather(g):
        for panel in range(3):
            flags = jnp.zeros((1, ORDER), jnp.int32)
            for k in range(MAXB):
                keep = (k < counts[g]) & (jnp.abs(blocks[g, k] // 16 - panel) <= 1)
                flags = jnp.where(list_id == k, jnp.where(keep, 1, 0), flags)
            valid[panel : panel + 1, :] = flags
            cut = slice(panel * SLAB, (panel + 1) * SLAB)
            turned[cut, :] = rows[g, :ORDER, cut].T

        def one_column(k, carry):
            p = blocks[g, k]
            there = pl.ds(pl.multiple_of(k * BLK, BLK), BLK)
            source = pl.ds(pl.multiple_of(p * BLK, BLK), BLK)
            keep = valid[pl.ds(p // 16, 1), :] + jnp.where(k < counts[g], 0, -1) > 0
            assembled[g, there, :] = jnp.where(keep, turned[source, :], 0.0)
            return carry

        lax.fori_loop(0, MAXB, one_column, 0, unroll=4)

    def scaled(g):
        whole_block = assembled[g]
        symmetric = 0.5 * (whole_block + whole_block.T)
        squares = jnp.sum(symmetric * symmetric, keepdims=True) + 1e-06
        size = jnp.full((1, 1), counts[g] * BLK, jnp.int32).astype(f32)
        return symmetric * (jnp.sqrt(size) / (2.0 * jnp.sqrt(squares)))

    def step(iterate):
        parts = split(iterate)
        return 1.5 * iterate - 0.5 * dot3(parts, split(dot3(parts, parts)))

    def thin(home, parts):
        high, low = split(home)
        both = dot(jnp.concatenate([high, low], axis=0), parts[0])
        return both[:BLK] + both[BLK:] + dot(high, parts[1])

    for g in range(2):
        gather(g)
    iterates = [step(iterate) for iterate in [scaled(g) for g in range(2)]]
    for g, iterate in enumerate(iterates):
        parts = split(iterate)
        home = iterate[:BLK]
        home = 1.5 * home - 0.5 * thin(thin(home, parts), parts)
        out[g * BLK : (g + 1) * BLK, :] = 0.5 * (jnp.where(row_id == col_id, 1.0, 0.0) - home)


def back_kernel(blocks, places, *refs):
    pieces, (win_hi, win_lo, mask, own, up, down, rows, full, part_hi, part_lo) = refs[:8], refs[8:]
    for n, piece in enumerate(pieces):
        rows[n * 2 * BLK : (n + 1) * 2 * BLK, :] = piece[...]
    dot = functools.partial(jnp.dot, preferred_element_type=f32)
    width = part_hi.shape[0]

    def some_blocks(step, carry):
        for slot in range(width):
            e = step * width + slot
            g = places[e]
            for i in range(MAXB):
                source = pl.ds(pl.multiple_of(blocks[e, i] * BLK, BLK), BLK)
                target = slice(i * BLK, (i + 1) * BLK)
                part_hi[slot, target, :] = win_hi[source, :]
                part_lo[slot, target, :] = win_lo[source, :]
            high, low = split(rows[pl.ds(pl.multiple_of(e * BLK, BLK), BLK), :])
            both = dot(jnp.concatenate([high, low], axis=0), part_hi[slot])
            there = pl.ds(pl.multiple_of(g * BLK, BLK), BLK)
            total = both[:BLK] + both[BLK:] + dot(high, part_lo[slot])
            full[there, :] = total * mask[there, :]
        return carry

    lax.fori_loop(0, SLAB // BLK // width, some_blocks, 0)
    send_parts(full[...], own, up, down)


def final_kernel(packed, density, charges):
    half = CHUNK // 2
    first = lax.broadcasted_iota(jnp.int32, (CHUNK, 128), 1) < CHUNK
    total = jnp.zeros((CHUNK, 128), f32)
    for m in range(SLAB // (2 * CHUNK)):
        a, b = packed[2 * m], packed[2 * m + 1]
        ab, bb = a[:CHUNK], b[:CHUNK]
        a2, b2 = a[CHUNK:], b[CHUNK:]
        left = jnp.where(first, ab, pltpu.roll(bb, CHUNK, 1))
        middle = jnp.where(first, pltpu.roll(ab, CHUNK, 1), bb)
        right = jnp.concatenate(
            [
                jnp.where(first[:half], a2, pltpu.roll(b2, CHUNK, 1)),
                jnp.where(first[:half], pltpu.roll(a2, CHUNK, 1), b2),
            ],
            axis=0,
        )
        for j, part in enumerate((left, middle, right)):
            density[:, j * SLAB + m * 128 : j * SLAB + (m + 1) * 128] = part
        total += left + middle + right
    charges[...] = jnp.sum(total.T, axis=0, keepdims=True)


def shards(hamiltonian, root, pattern, sub_blocks, sub_count):
    sds = jax.ShapeDtypeStruct
    slab = lax.axis_index("rows")
    col, core = lax.axis_index("cols"), lax.axis_index("space")
    home = 2 * col + core
    parts = (sds((SLAB, LANES), f32), sds((SLAB, 2 * CHUNK), f32), sds((SLAB, 2 * CHUNK), f32))
    product = dict(flops=6 * SLAB * 3 * SLAB * LANES, moved=6 << 20)

    with jax.named_scope("inputs"):
        extra = jnp.pad(sub_blocks.astype(f32), ((0, 6), (0, 3 * SLAB - MAXB)))
        ham = shared(jnp.concatenate([hamiltonian, extra], axis=0))
        chips = jnp.stack([col, (col + 3) % 4, (col + 1) % 4, (col + 2) % 4])
        order = jnp.concatenate([2 * chips + core, 2 * chips + 1 - core]).astype(jnp.int32)
        places = (2 * order[:, None] + jnp.arange(2, dtype=jnp.int32)[None, :]).reshape(-1)
        pieces = [lax.dynamic_slice(root, (0, j * SLAB + home * CHUNK), (SLAB, CHUNK)) for j in range(3)]
        above = passed_along(jnp.concatenate(pieces[1:], axis=1), "rows", 1)
        below = passed_along(jnp.concatenate(pieces[:2], axis=1), "rows", -1)
        own = jnp.concatenate(pieces + [jnp.zeros((SLAB, CHUNK), f32)], axis=1)
        mask = lax.dynamic_slice(pattern, (slab * 16, 0), (16, 48)).astype(f32).reshape(16, 3, 16)
        mask = lax.dynamic_slice(mask, (0, 0, 2 * home), (16, 3, 2)).reshape(16, 6)
        mask = jnp.pad(mask, ((0, 0), (0, 2)))
        mask = jnp.broadcast_to(mask[:, None, :, None], (16, BLK, 8, BLK)).reshape(SLAB, LANES)
        root_hi, root_lo, win_hi, win_lo = kernel_call(
            split_kernel,
            (sds((SLAB, 3 * SLAB), bf16),) * 2 + (sds((3 * SLAB, LANES), bf16),) * 2,
            (root, above, own, below),
            [VMEM] * 4,
            flops=1 << 22,
            moved=8 << 20,
        )
    with jax.named_scope("half_done"):
        own, up, down, lists = kernel_call(
            first_kernel,
            parts + (sds((2 * SLAB // CHUNK, 128), jnp.int32),),
            (order,) + ham + (win_hi, win_lo, mask),
            [SMEM] + [VMEM] * 11,
            scratch=[pltpu.VMEM((SLAB, 3 * SLAB), bf16)] * 2,
            limit=16,
            **product,
        )
        above, below = passed_along(up, "rows", 1), passed_along(down, "rows", -1)
    with jax.named_scope("orthogonal"):
        mine, up, down = kernel_call(
            ortho_kernel,
            (sds((3 * CHUNK, SLAB), f32), sds((2 * CHUNK, SLAB), f32), sds((2 * CHUNK, SLAB), f32)),
            (root_hi, root_lo, above, own, below, mask),
            [VMEM] * 6,
            **product,
        )
        above, below = passed_along(up, "rows", 1), passed_along(down, "rows", -1)
        whole = around(mine)
        far = passed_along(mine, "cols", 2)
        above = (above,) + around(above)[1:] + (passed_along(far[CHUNK:], "rows", 1),)
        below = (below,) + around(below)[1:] + (passed_along(far[: 2 * CHUNK], "rows", -1),)
        window = swapped(whole + (far,)) + swapped(above) + swapped(below)
    with jax.named_scope("solve"):
        rows = kernel_call(
            solve_kernel,
            sds((2 * BLK, ORDER), f32),
            (sub_blocks, sub_count, order) + window,
            [SMEM] * 3 + [VMEM] * 24,
            scratch=[
                pltpu.SMEM((2, 3 * 16), jnp.int32),
                pltpu.VMEM((2, ORDER + BLK, 3 * SLAB), f32),
                pltpu.VMEM((3 * SLAB, ORDER), f32),
                pltpu.VMEM((2, ORDER, ORDER), f32),
                pltpu.VMEM((8, ORDER), jnp.int32),
            ],
            limit=24,
            flops=12 * ORDER**3,
            moved=8 << 20,
        )
    with jax.named_scope("share"):
        rows = shared(rows)
    with jax.named_scope("half_back"):
        own, up, down = kernel_call(
            back_kernel,
            parts,
            (lists, places) + rows + (win_hi, win_lo, mask),
            [SMEM, SMEM] + [VMEM] * 11,
            scratch=[
                pltpu.VMEM((SLAB, ORDER), f32),
                pltpu.VMEM((SLAB, LANES), f32),
                pltpu.VMEM((4, ORDER, LANES), bf16),
                pltpu.VMEM((4, ORDER, LANES), bf16),
            ],
            **product,
        )
        above, below = passed_along(up, "rows", 1), passed_along(down, "rows", -1)
    with jax.named_scope("density"):
        packed = kernel_call(
            density_kernel,
            sds((SLAB // CHUNK, 3 * CHUNK // 2, 2 * CHUNK), f32),
            (root_hi, root_lo, above, own, below, mask),
            [VMEM] * 6,
            **product,
        )
        packed = lax.all_to_all(packed, ALL, 0, 0)
        density, charges = kernel_call(
            final_kernel,
            (sds((CHUNK, 3 * SLAB), f32), sds((1, CHUNK), f32)),
            (packed,),
            [VMEM],
            flops=1 << 20,
            moved=1 << 20,
        )
    return density, charges.reshape(CHUNK)


def solution(mesh):
    return jax.shard_map(
        shards,
        mesh=mesh,
        in_specs=(
            P(("rows", "cols", "space"), None),
            P("rows", None),
            P(),
            P(("rows", "cols", "space"), None),
            P(("rows", "cols", "space")),
        ),
        out_specs=(P(("rows", "cols", "space"), None), P(("rows", "cols", "space"))),
        check_vma=False,
    )
```

```python
import functools

import jax
import jax.numpy as jnp
from jax import lax
from jax.experimental import pallas as pl
from jax.experimental.pallas import tpu as pltpu
from jax.sharding import PartitionSpec as P

BLK = 32
MAXB = 16
SLAB = 512
CHUNK = 64
LANES = 256
ORDER = MAXB * BLK
f32 = jnp.float32
bf16 = jnp.bfloat16
ALL = ("cols", "space")
VMEM = pl.BlockSpec(memory_space=pltpu.VMEM)
SMEM = pl.BlockSpec(memory_space=pltpu.SMEM)


def passed_along(value, axis, steps):
    count = lax.axis_size(axis)
    pairs = [(source, (source + steps) % count) for source in range(count)]
    return lax.ppermute(value, axis, pairs)


def around(value):
    return value, passed_along(value, "cols", 1), passed_along(value, "cols", -1)


def swapped(values):
    return values + tuple(passed_along(value, "space", 1) for value in values)


def shared(value):
    return swapped(lax.optimization_barrier(around(value) + (passed_along(value, "cols", 2),)))


def kernel_call(body, shapes, operands, in_specs, scratch=(), limit=12, flops=0, moved=0):
    return pl.pallas_call(
        body,
        out_shape=shapes,
        in_specs=in_specs,
        out_specs=jax.tree.map(lambda _: VMEM, shapes),
        scratch_shapes=list(scratch),
        compiler_params=pltpu.CompilerParams(vmem_limit_bytes=limit << 20),
        cost_estimate=pl.CostEstimate(flops=flops, bytes_accessed=moved, transcendentals=0),
    )(*operands)


def split(x):
    high = x.astype(bf16)
    return high, (x - high.astype(f32)).astype(bf16)


def dot3(a, b):
    dot = functools.partial(jnp.dot, preferred_element_type=f32)
    return dot(a[0], b[0]) + (dot(a[0], b[1]) + dot(a[1], b[0]))


def send_parts(full, own, up, down):
    own[...] = full
    up[...] = pltpu.roll(full, LANES - CHUNK, 1)[:, : 2 * CHUNK]
    down[...] = full[:, : 2 * CHUNK]


def window_parts(above, own, below):
    blank = jnp.zeros((SLAB, 2 * CHUNK), f32)
    return (
        jnp.concatenate([above, blank], axis=1),
        own,
        pltpu.roll(jnp.concatenate([below, blank], axis=1), CHUNK, 1),
    )


def split_kernel(root, above, own, below, root_hi, root_lo, win_hi, win_lo):
    root_hi[...], root_lo[...] = split(root[...])
    for k, part in enumerate(window_parts(above[...], own[...], below[...])):
        rows = slice(k * SLAB, (k + 1) * SLAB)
        win_hi[rows, :], win_lo[rows, :] = split(part)


def first_kernel(order, *refs):
    pieces, (win_hi, win_lo, mask, own, up, down, ham_hi, ham_lo) = refs[:8], refs[8:]
    for n, piece in enumerate(pieces):
        there = pl.ds(pl.multiple_of(order[n] * CHUNK, CHUNK), CHUNK)
        ham_hi[there, :], ham_lo[there, :] = split(piece[...])
    total = jnp.zeros((SLAB, LANES), f32)
    for k in range(3):
        cut = slice(k * SLAB, (k + 1) * SLAB)
        total += dot3((ham_hi[:, cut], ham_lo[:, cut]), (win_hi[cut, :], win_lo[cut, :]))
    send_parts(total * mask[...], own, up, down)


def root_product(root_hi, root_lo, above, own, below, mask):
    total = jnp.zeros((SLAB, LANES), f32)
    for k, part in enumerate(window_parts(above[...], own[...], below[...])):
        cut = slice(k * SLAB, (k + 1) * SLAB)
        total += dot3((root_hi[:, cut], root_lo[:, cut]), split(part))
    return total * mask[...]


def ortho_kernel(blocks, root_hi, root_lo, above, own, below, mask, mine, up, down):
    turned = root_product(root_hi, root_lo, above, own, below, mask).T
    mine[: 3 * CHUNK, :] = turned[: 3 * CHUNK]
    line = lax.broadcasted_iota(jnp.int32, (8, SLAB), 0)
    lane = lax.broadcasted_iota(jnp.int32, (8, SLAB), 1)
    lists = jnp.zeros((8, SLAB), jnp.int32)
    for g in range(2):
        for i in range(MAXB):
            lists = jnp.where((line == g) & (lane == i), blocks[g, i], lists)
    mine[3 * CHUNK :, :] = lists.astype(f32)
    up[...] = turned[CHUNK : 3 * CHUNK]
    down[...] = turned[: 2 * CHUNK]


def density_kernel(root_hi, root_lo, above, own, below, mask, packed):
    full = root_product(root_hi, root_lo, above, own, below, mask)
    half = CHUNK // 2
    for c in range(SLAB // CHUNK):
        rows = full[c * CHUNK : (c + 1) * CHUNK]
        packed[c, :CHUNK, :] = rows[:, : 2 * CHUNK]
        last = rows[:, 2 * CHUNK :]
        lane = lax.broadcasted_iota(jnp.int32, (half, 2 * CHUNK), 1)
        packed[c, CHUNK:, :] = jnp.where(lane < CHUNK, last[:half], pltpu.roll(last[half:], CHUNK, 1))


def solve_kernel(blocks, counts, order, *refs):
    pieces, (out, lists, inverse, rows, turned, assembled, valid) = refs[:24], refs[24:]
    row_id = lax.broadcasted_iota(jnp.int32, (BLK, ORDER), 0)
    col_id = lax.broadcasted_iota(jnp.int32, (BLK, ORDER), 1)
    list_id = lax.broadcasted_iota(jnp.int32, (1, ORDER), 1) // BLK
    dot = functools.partial(jnp.dot, preferred_element_type=f32)

    for g in range(2):
        for q in range(3 * 16):
            inverse[g, q] = MAXB
        for k in range(MAXB):
            inverse[g, blocks[g, k]] = k
    for n in range(8):
        lists[2 * n : 2 * n + 2, :] = pieces[n][3 * CHUNK : 3 * CHUNK + 2, :128].astype(jnp.int32)
        for panel, piece, first in ((1, pieces[n], 0), (0, pieces[8 + n], 0), (2, pieces[16 + n], 1)):
            for at in range(6 if panel == 1 else 4):
                q = (first + at // 2) * 16 + 2 * order[n] + at % 2
                block = piece[at * BLK : (at + 1) * BLK, :]
                for g in range(2):
                    there = pl.ds(pl.multiple_of(inverse[g, q] * BLK, BLK), BLK)
                    rows[g, there, panel * SLAB : (panel + 1) * SLAB] = block

    def gather(g):
        for panel in range(3):
            flags = jnp.zeros((1, ORDER), jnp.int32)
            for k in range(MAXB):
                keep = (k < counts[g]) & (jnp.abs(blocks[g, k] // 16 - panel) <= 1)
                flags = jnp.where(list_id == k, jnp.where(keep, 1, 0), flags)
            valid[panel : panel + 1, :] = flags
            cut = slice(panel * SLAB, (panel + 1) * SLAB)
            turned[cut, :] = rows[g, :ORDER, cut].T

        def one_column(k, carry):
            p = blocks[g, k]
            there = pl.ds(pl.multiple_of(k * BLK, BLK), BLK)
            source = pl.ds(pl.multiple_of(p * BLK, BLK), BLK)
            keep = valid[pl.ds(p // 16, 1), :] + jnp.where(k < counts[g], 0, -1) > 0
            assembled[g, there, :] = jnp.where(keep, turned[source, :], 0.0)
            return carry

        lax.fori_loop(0, MAXB, one_column, 0, unroll=4)

    def scaled(g):
        whole_block = assembled[g]
        symmetric = 0.5 * (whole_block + whole_block.T)
        squares = jnp.sum(symmetric * symmetric, keepdims=True) + 1e-06
        size = jnp.full((1, 1), counts[g] * BLK, jnp.int32).astype(f32)
        return symmetric * (jnp.sqrt(size) / (2.0 * jnp.sqrt(squares)))

    def step(iterate):
        parts = split(iterate)
        return 1.5 * iterate - 0.5 * dot3(parts, split(dot3(parts, parts)))

    def thin(home, parts):
        high, low = split(home)
        both = dot(jnp.concatenate([high, low], axis=0), parts[0])
        return both[:BLK] + both[BLK:] + dot(high, parts[1])

    for g in range(2):
        gather(g)
    iterates = [step(iterate) for iterate in [scaled(g) for g in range(2)]]
    for g, iterate in enumerate(iterates):
        parts = split(iterate)
        home = iterate[:BLK]
        home = 1.5 * home - 0.5 * thin(thin(home, parts), parts)
        out[g * BLK : (g + 1) * BLK, :] = 0.5 * (jnp.where(row_id == col_id, 1.0, 0.0) - home)


def back_kernel(blocks, places, *refs):
    pieces, (win_hi, win_lo, mask, own, up, down, rows, full, part_hi, part_lo) = refs[:8], refs[8:]
    for n, piece in enumerate(pieces):
        rows[n * 2 * BLK : (n + 1) * 2 * BLK, :] = piece[...]
    dot = functools.partial(jnp.dot, preferred_element_type=f32)
    width = part_hi.shape[0]

    def some_blocks(step, carry):
        for slot in range(width):
            e = step * width + slot
            g = places[e]
            for i in range(MAXB):
                source = pl.ds(pl.multiple_of(blocks[e, i] * BLK, BLK), BLK)
                target = slice(i * BLK, (i + 1) * BLK)
                part_hi[slot, target, :] = win_hi[source, :]
                part_lo[slot, target, :] = win_lo[source, :]
            high, low = split(rows[pl.ds(pl.multiple_of(e * BLK, BLK), BLK), :])
            both = dot(jnp.concatenate([high, low], axis=0), part_hi[slot])
            there = pl.ds(pl.multiple_of(g * BLK, BLK), BLK)
            total = both[:BLK] + both[BLK:] + dot(high, part_lo[slot])
            full[there, :] = total * mask[there, :]
        return carry

    lax.fori_loop(0, SLAB // BLK // width, some_blocks, 0)
    send_parts(full[...], own, up, down)


def final_kernel(packed, density, charges):
    half = CHUNK // 2
    first = lax.broadcasted_iota(jnp.int32, (CHUNK, 128), 1) < CHUNK
    total = jnp.zeros((CHUNK, 128), f32)
    for m in range(SLAB // (2 * CHUNK)):
        a, b = packed[2 * m], packed[2 * m + 1]
        ab, bb = a[:CHUNK], b[:CHUNK]
        a2, b2 = a[CHUNK:], b[CHUNK:]
        left = jnp.where(first, ab, pltpu.roll(bb, CHUNK, 1))
        middle = jnp.where(first, pltpu.roll(ab, CHUNK, 1), bb)
        right = jnp.concatenate(
            [
                jnp.where(first[:half], a2, pltpu.roll(b2, CHUNK, 1)),
                jnp.where(first[:half], pltpu.roll(a2, CHUNK, 1), b2),
            ],
            axis=0,
        )
        for j, part in enumerate((left, middle, right)):
            density[:, j * SLAB + m * 128 : j * SLAB + (m + 1) * 128] = part
        total += left + middle + right
    charges[...] = jnp.sum(total.T, axis=0, keepdims=True)


def shards(hamiltonian, root, pattern, sub_blocks, sub_count):
    sds = jax.ShapeDtypeStruct
    slab = lax.axis_index("rows")
    col, core = lax.axis_index("cols"), lax.axis_index("space")
    home = 2 * col + core
    parts = (sds((SLAB, LANES), f32), sds((SLAB, 2 * CHUNK), f32), sds((SLAB, 2 * CHUNK), f32))
    product = dict(flops=6 * SLAB * 3 * SLAB * LANES, moved=6 << 20)

    with jax.named_scope("inputs"):
        chips = jnp.stack([col, (col + 3) % 4, (col + 1) % 4, (col + 2) % 4])
        order = jnp.concatenate([2 * chips + core, 2 * chips + 1 - core]).astype(jnp.int32)
        places = (2 * order[:, None] + jnp.arange(2, dtype=jnp.int32)[None, :]).reshape(-1)
        pieces = [lax.dynamic_slice(root, (0, j * SLAB + home * CHUNK), (SLAB, CHUNK)) for j in range(3)]
        above = passed_along(jnp.concatenate(pieces[1:], axis=1), "rows", 1)
        below = passed_along(jnp.concatenate(pieces[:2], axis=1), "rows", -1)
        ham = around(hamiltonian) + (passed_along(hamiltonian, "cols", 2),)
        above, below, ham = lax.optimization_barrier((above, below, ham))
        ham = swapped(ham)
        own = jnp.concatenate(pieces + [jnp.zeros((SLAB, CHUNK), f32)], axis=1)
        mask = lax.dynamic_slice(pattern, (slab * 16, 0), (16, 48)).astype(f32).reshape(16, 3, 16)
        mask = lax.dynamic_slice(mask, (0, 0, 2 * home), (16, 3, 2)).reshape(16, 6)
        mask = jnp.pad(mask, ((0, 0), (0, 2)))
        mask = jnp.broadcast_to(mask[:, None, :, None], (16, BLK, 8, BLK)).reshape(SLAB, LANES)
        root_hi, root_lo, win_hi, win_lo = kernel_call(
            split_kernel,
            (sds((SLAB, 3 * SLAB), bf16),) * 2 + (sds((3 * SLAB, LANES), bf16),) * 2,
            (root, above, own, below),
            [VMEM] * 4,
            flops=1 << 22,
            moved=8 << 20,
        )
    with jax.named_scope("half_done"):
        own, up, down = kernel_call(
            first_kernel,
            parts,
            (order,) + ham + (win_hi, win_lo, mask),
            [SMEM] + [VMEM] * 11,
            scratch=[pltpu.VMEM((SLAB, 3 * SLAB), bf16)] * 2,
            limit=16,
            **product,
        )
        above, below = passed_along(up, "rows", 1), passed_along(down, "rows", -1)
    with jax.named_scope("orthogonal"):
        mine, up, down = kernel_call(
            ortho_kernel,
            (sds((3 * CHUNK + 8, SLAB), f32),) + (sds((2 * CHUNK, SLAB), f32),) * 2,
            (sub_blocks, root_hi, root_lo, above, own, below, mask),
            [SMEM] + [VMEM] * 6,
            **product,
        )
        above, below = passed_along(up, "rows", 1), passed_along(down, "rows", -1)
        _, before, after = around(mine)
        far = passed_along(mine, "cols", 2)
        above, below = lax.optimization_barrier((above, below))
        above, below = around(above), around(below)
        above += (passed_along(far[CHUNK : 3 * CHUNK], "rows", 1),)
        below += (passed_along(far[: 2 * CHUNK], "rows", -1),)
        whole = lax.optimization_barrier((mine, before, after, far))
        window = swapped(whole) + swapped(above) + swapped(below)
    with jax.named_scope("solve"):
        rows, lists = kernel_call(
            solve_kernel,
            (sds((2 * BLK, ORDER), f32), sds((2 * SLAB // CHUNK, 128), jnp.int32)),
            (sub_blocks, sub_count, order) + window,
            [SMEM] * 3 + [VMEM] * 24,
            scratch=[
                pltpu.SMEM((2, 3 * 16), jnp.int32),
                pltpu.VMEM((2, ORDER + BLK, 3 * SLAB), f32),
                pltpu.VMEM((3 * SLAB, ORDER), f32),
                pltpu.VMEM((2, ORDER, ORDER), f32),
                pltpu.VMEM((8, ORDER), jnp.int32),
            ],
            limit=24,
            flops=12 * ORDER**3,
            moved=8 << 20,
        )
    with jax.named_scope("share"):
        rows = shared(rows)
    with jax.named_scope("half_back"):
        own, up, down = kernel_call(
            back_kernel,
            parts,
            (lists, places) + rows + (win_hi, win_lo, mask),
            [SMEM, SMEM] + [VMEM] * 11,
            scratch=[
                pltpu.VMEM((SLAB, ORDER), f32),
                pltpu.VMEM((SLAB, LANES), f32),
                pltpu.VMEM((4, ORDER, LANES), bf16),
                pltpu.VMEM((4, ORDER, LANES), bf16),
            ],
            **product,
        )
        above, below = passed_along(up, "rows", 1), passed_along(down, "rows", -1)
    with jax.named_scope("density"):
        packed = kernel_call(
            density_kernel,
            sds((SLAB // CHUNK, 3 * CHUNK // 2, 2 * CHUNK), f32),
            (root_hi, root_lo, above, own, below, mask),
            [VMEM] * 6,
            **product,
        )
        packed = lax.all_to_all(packed, ALL, 0, 0)
        density, charges = kernel_call(
            final_kernel,
            (sds((CHUNK, 3 * SLAB), f32), sds((1, CHUNK), f32)),
            (packed,),
            [VMEM],
            flops=1 << 20,
            moved=1 << 20,
        )
    return density, charges.reshape(CHUNK)


def solution(mesh):
    return jax.shard_map(
        shards,
        mesh=mesh,
        in_specs=(
            P(("rows", "cols", "space"), None),
            P("rows", None),
            P(),
            P(("rows", "cols", "space"), None),
            P(("rows", "cols", "space")),
        ),
        out_specs=(P(("rows", "cols", "space"), None), P(("rows", "cols", "space"))),
        check_vma=False,
    )
```

```python
import functools

import jax
import jax.numpy as jnp
from jax import lax
from jax.experimental import pallas as pl
from jax.experimental.pallas import tpu as pltpu
from jax.sharding import PartitionSpec as P

BLK = 32
MAXB = 16
SLAB = 512
CHUNK = 64
LANES = 256
ORDER = MAXB * BLK
f32 = jnp.float32
bf16 = jnp.bfloat16
ALL = ("cols", "space")
VMEM = pl.BlockSpec(memory_space=pltpu.VMEM)
SMEM = pl.BlockSpec(memory_space=pltpu.SMEM)


def passed_along(value, axis, steps):
    count = lax.axis_size(axis)
    pairs = [(source, (source + steps) % count) for source in range(count)]
    return lax.ppermute(value, axis, pairs)


def around(value):
    return value, passed_along(value, "cols", 1), passed_along(value, "cols", -1)


def swapped(values):
    return values + tuple(passed_along(value, "space", 1) for value in values)


def shared(value):
    return swapped(lax.optimization_barrier(around(value) + (passed_along(value, "cols", 2),)))


def kernel_call(body, shapes, operands, in_specs, scratch=(), limit=12, flops=0, moved=0):
    return pl.pallas_call(
        body,
        out_shape=shapes,
        in_specs=in_specs,
        out_specs=jax.tree.map(lambda _: VMEM, shapes),
        scratch_shapes=list(scratch),
        compiler_params=pltpu.CompilerParams(vmem_limit_bytes=limit << 20),
        cost_estimate=pl.CostEstimate(flops=flops, bytes_accessed=moved, transcendentals=0),
    )(*operands)


def split(x):
    high = x.astype(bf16)
    return high, (x - high.astype(f32)).astype(bf16)


def dot3(a, b):
    dot = functools.partial(jnp.dot, preferred_element_type=f32)
    return dot(a[0], b[0]) + (dot(a[0], b[1]) + dot(a[1], b[0]))


def send_parts(full, own, up, down):
    own[...] = full
    up[...] = pltpu.roll(full, LANES - CHUNK, 1)[:, : 2 * CHUNK]
    down[...] = full[:, : 2 * CHUNK]


def window_parts(above, own, below):
    blank = jnp.zeros((SLAB, 2 * CHUNK), f32)
    return (
        jnp.concatenate([above, blank], axis=1),
        own,
        pltpu.roll(jnp.concatenate([below, blank], axis=1), CHUNK, 1),
    )


def split_kernel(root, root_hi, root_lo):
    root_hi[...], root_lo[...] = split(root[...])


def first_kernel(order, *refs):
    pieces, refs = refs[:8], refs[8:]
    above, mine, below, mask, own, up, down, win_hi, win_lo, ham_hi, ham_lo = refs
    for k, part in enumerate(window_parts(above[...], mine[...], below[...])):
        cut = slice(k * SLAB, (k + 1) * SLAB)
        win_hi[cut, :], win_lo[cut, :] = split(part)
    for n, piece in enumerate(pieces):
        there = pl.ds(pl.multiple_of(order[n] * CHUNK, CHUNK), CHUNK)
        ham_hi[there, :], ham_lo[there, :] = split(piece[...])
    total = jnp.zeros((SLAB, LANES), f32)
    for k in range(3):
        cut = slice(k * SLAB, (k + 1) * SLAB)
        total += dot3((ham_hi[:, cut], ham_lo[:, cut]), (win_hi[cut, :], win_lo[cut, :]))
    send_parts(total * mask[...], own, up, down)


def root_product(root_hi, root_lo, above, own, below, mask):
    total = jnp.zeros((SLAB, LANES), f32)
    for k, part in enumerate(window_parts(above[...], own[...], below[...])):
        cut = slice(k * SLAB, (k + 1) * SLAB)
        total += dot3((root_hi[:, cut], root_lo[:, cut]), split(part))
    return total * mask[...]


def ortho_kernel(blocks, root_hi, root_lo, above, own, below, mask, mine, up, down):
    turned = root_product(root_hi, root_lo, above, own, below, mask).T
    mine[: 3 * CHUNK, :] = turned[: 3 * CHUNK]
    line = lax.broadcasted_iota(jnp.int32, (8, SLAB), 0)
    lane = lax.broadcasted_iota(jnp.int32, (8, SLAB), 1)
    lists = jnp.zeros((8, SLAB), jnp.int32)
    for g in range(2):
        for i in range(MAXB):
            lists = jnp.where((line == g) & (lane == i), blocks[g, i], lists)
    mine[3 * CHUNK :, :] = lists.astype(f32)
    up[...] = turned[CHUNK : 3 * CHUNK]
    down[...] = turned[: 2 * CHUNK]


def density_kernel(root_hi, root_lo, above, own, below, mask, packed):
    full = root_product(root_hi, root_lo, above, own, below, mask)
    half = CHUNK // 2
    for c in range(SLAB // CHUNK):
        rows = full[c * CHUNK : (c + 1) * CHUNK]
        packed[c, :CHUNK, :] = rows[:, : 2 * CHUNK]
        last = rows[:, 2 * CHUNK :]
        lane = lax.broadcasted_iota(jnp.int32, (half, 2 * CHUNK), 1)
        packed[c, CHUNK:, :] = jnp.where(lane < CHUNK, last[:half], pltpu.roll(last[half:], CHUNK, 1))


def solve_kernel(blocks, counts, order, *refs):
    pieces, (out, lists, inverse, rows, turned, assembled, valid) = refs[:24], refs[24:]
    row_id = lax.broadcasted_iota(jnp.int32, (BLK, ORDER), 0)
    col_id = lax.broadcasted_iota(jnp.int32, (BLK, ORDER), 1)
    list_id = lax.broadcasted_iota(jnp.int32, (1, ORDER), 1) // BLK
    dot = functools.partial(jnp.dot, preferred_element_type=f32)

    for g in range(2):
        for q in range(3 * 16):
            inverse[g, q] = MAXB
        for k in range(MAXB):
            inverse[g, blocks[g, k]] = k
    for n in range(8):
        lists[2 * n : 2 * n + 2, :] = pieces[n][3 * CHUNK : 3 * CHUNK + 2, :128].astype(jnp.int32)
        for panel, piece, first in ((1, pieces[n], 0), (0, pieces[8 + n], 0), (2, pieces[16 + n], 1)):
            for at in range(6 if panel == 1 else 4):
                q = (first + at // 2) * 16 + 2 * order[n] + at % 2
                block = piece[at * BLK : (at + 1) * BLK, :]
                for g in range(2):
                    there = pl.ds(pl.multiple_of(inverse[g, q] * BLK, BLK), BLK)
                    rows[g, there, panel * SLAB : (panel + 1) * SLAB] = block

    def gather(g):
        for panel in range(3):
            flags = jnp.zeros((1, ORDER), jnp.int32)
            for k in range(MAXB):
                keep = (k < counts[g]) & (jnp.abs(blocks[g, k] // 16 - panel) <= 1)
                flags = jnp.where(list_id == k, jnp.where(keep, 1, 0), flags)
            valid[panel : panel + 1, :] = flags
            cut = slice(panel * SLAB, (panel + 1) * SLAB)
            turned[cut, :] = rows[g, :ORDER, cut].T

        def one_column(k, carry):
            p = blocks[g, k]
            there = pl.ds(pl.multiple_of(k * BLK, BLK), BLK)
            source = pl.ds(pl.multiple_of(p * BLK, BLK), BLK)
            keep = valid[pl.ds(p // 16, 1), :] + jnp.where(k < counts[g], 0, -1) > 0
            assembled[g, there, :] = jnp.where(keep, turned[source, :], 0.0)
            return carry

        lax.fori_loop(0, MAXB, one_column, 0, unroll=4)

    def scaled(g):
        whole_block = assembled[g]
        symmetric = 0.5 * (whole_block + whole_block.T)
        squares = jnp.sum(symmetric * symmetric, keepdims=True) + 1e-06
        size = jnp.full((1, 1), counts[g] * BLK, jnp.int32).astype(f32)
        return symmetric * (jnp.sqrt(size) / (2.0 * jnp.sqrt(squares)))

    def step(iterate):
        parts = split(iterate)
        return 1.5 * iterate - 0.5 * dot3(parts, split(dot3(parts, parts)))

    def thin(home, parts):
        high, low = split(home)
        both = dot(jnp.concatenate([high, low], axis=0), parts[0])
        return both[:BLK] + both[BLK:] + dot(high, parts[1])

    for g in range(2):
        gather(g)
    iterates = [step(iterate) for iterate in [scaled(g) for g in range(2)]]
    for g, iterate in enumerate(iterates):
        parts = split(iterate)
        home = iterate[:BLK]
        home = 1.5 * home - 0.5 * thin(thin(home, parts), parts)
        out[g * BLK : (g + 1) * BLK, :] = 0.5 * (jnp.where(row_id == col_id, 1.0, 0.0) - home)


def back_kernel(blocks, places, *refs):
    pieces, (win_hi, win_lo, mask, own, up, down, rows, full, part_hi, part_lo) = refs[:8], refs[8:]
    for n, piece in enumerate(pieces):
        rows[n * 2 * BLK : (n + 1) * 2 * BLK, :] = piece[...]
    dot = functools.partial(jnp.dot, preferred_element_type=f32)
    width = part_hi.shape[0]

    def some_blocks(step, carry):
        for slot in range(width):
            e = step * width + slot
            g = places[e]
            for i in range(MAXB):
                source = pl.ds(pl.multiple_of(blocks[e, i] * BLK, BLK), BLK)
                target = slice(i * BLK, (i + 1) * BLK)
                part_hi[slot, target, :] = win_hi[source, :]
                part_lo[slot, target, :] = win_lo[source, :]
            high, low = split(rows[pl.ds(pl.multiple_of(e * BLK, BLK), BLK), :])
            both = dot(jnp.concatenate([high, low], axis=0), part_hi[slot])
            there = pl.ds(pl.multiple_of(g * BLK, BLK), BLK)
            total = both[:BLK] + both[BLK:] + dot(high, part_lo[slot])
            full[there, :] = total * mask[there, :]
        return carry

    lax.fori_loop(0, SLAB // BLK // width, some_blocks, 0)
    send_parts(full[...], own, up, down)


def final_kernel(packed, density, charges):
    half = CHUNK // 2
    first = lax.broadcasted_iota(jnp.int32, (CHUNK, 128), 1) < CHUNK
    total = jnp.zeros((CHUNK, 128), f32)
    for m in range(SLAB // (2 * CHUNK)):
        a, b = packed[2 * m], packed[2 * m + 1]
        ab, bb = a[:CHUNK], b[:CHUNK]
        a2, b2 = a[CHUNK:], b[CHUNK:]
        left = jnp.where(first, ab, pltpu.roll(bb, CHUNK, 1))
        middle = jnp.where(first, pltpu.roll(ab, CHUNK, 1), bb)
        right = jnp.concatenate(
            [
                jnp.where(first[:half], a2, pltpu.roll(b2, CHUNK, 1)),
                jnp.where(first[:half], pltpu.roll(a2, CHUNK, 1), b2),
            ],
            axis=0,
        )
        for j, part in enumerate((left, middle, right)):
            density[:, j * SLAB + m * 128 : j * SLAB + (m + 1) * 128] = part
        total += left + middle + right
    charges[...] = jnp.sum(total.T, axis=0, keepdims=True)


def shards(hamiltonian, root, pattern, sub_blocks, sub_count):
    sds = jax.ShapeDtypeStruct
    slab = lax.axis_index("rows")
    col, core = lax.axis_index("cols"), lax.axis_index("space")
    home = 2 * col + core
    parts = (sds((SLAB, LANES), f32), sds((SLAB, 2 * CHUNK), f32), sds((SLAB, 2 * CHUNK), f32))
    product = dict(flops=6 * SLAB * 3 * SLAB * LANES, moved=6 << 20)

    with jax.named_scope("inputs"):
        chips = jnp.stack([col, (col + 3) % 4, (col + 1) % 4, (col + 2) % 4])
        order = jnp.concatenate([2 * chips + core, 2 * chips + 1 - core]).astype(jnp.int32)
        places = (2 * order[:, None] + jnp.arange(2, dtype=jnp.int32)[None, :]).reshape(-1)
        pieces = [lax.dynamic_slice(root, (0, j * SLAB + home * CHUNK), (SLAB, CHUNK)) for j in range(3)]
        above = passed_along(jnp.concatenate(pieces[1:], axis=1), "rows", 1)
        below = passed_along(jnp.concatenate(pieces[:2], axis=1), "rows", -1)
        ham = around(hamiltonian) + (passed_along(hamiltonian, "cols", 2),)
        own = jnp.concatenate(pieces + [jnp.zeros((SLAB, CHUNK), f32)], axis=1)
        mask = lax.dynamic_slice(pattern, (slab * 16, 0), (16, 48)).astype(f32).reshape(16, 3, 16)
        mask = lax.dynamic_slice(mask, (0, 0, 2 * home), (16, 3, 2)).reshape(16, 6)
        mask = jnp.pad(mask, ((0, 0), (0, 2)))
        mask = jnp.broadcast_to(mask[:, None, :, None], (16, BLK, 8, BLK)).reshape(SLAB, LANES)
        root_hi, root_lo = kernel_call(
            split_kernel,
            (sds((SLAB, 3 * SLAB), bf16),) * 2,
            (root,),
            [VMEM],
            limit=8,
            flops=1 << 22,
            moved=8 << 20,
        )
        chips = jnp.stack([col, (col + 3) % 4, (col + 1) % 4, (col + 2) % 4])
        order = jnp.concatenate([2 * chips + core, 2 * chips + 1 - core]).astype(jnp.int32)
        places = (2 * order[:, None] + jnp.arange(2, dtype=jnp.int32)[None, :]).reshape(-1)
        ready = (above, below, own, mask, root_hi, root_lo, order, places, ham)
        above, below, own, mask, root_hi, root_lo, order, places, ham = lax.optimization_barrier(ready)
        ham = swapped(ham)
    with jax.named_scope("half_done"):
        own, up, down, win_hi, win_lo = kernel_call(
            first_kernel,
            parts + (sds((3 * SLAB, LANES), bf16),) * 2,
            (order,) + ham + (above, own, below, mask),
            [SMEM] + [VMEM] * 12,
            scratch=[pltpu.VMEM((SLAB, 3 * SLAB), bf16)] * 2,
            limit=16,
            **product,
        )
        above, below = passed_along(up, "rows", 1), passed_along(down, "rows", -1)
    with jax.named_scope("orthogonal"):
        mine, up, down = kernel_call(
            ortho_kernel,
            (sds((3 * CHUNK + 8, SLAB), f32),) + (sds((2 * CHUNK, SLAB), f32),) * 2,
            (sub_blocks, root_hi, root_lo, above, own, below, mask),
            [SMEM] + [VMEM] * 6,
            **product,
        )
        above, below = passed_along(up, "rows", 1), passed_along(down, "rows", -1)
        _, before, after = around(mine)
        far = passed_along(mine, "cols", 2)
        above, before = lax.optimization_barrier((above, before))
        below, after = lax.optimization_barrier((below, after))
        above, below = around(above), around(below)
        above += (passed_along(far[CHUNK : 3 * CHUNK], "rows", 1),)
        below += (passed_along(far[: 2 * CHUNK], "rows", -1),)
        whole = lax.optimization_barrier((mine, before, after, far))
        window = swapped(whole) + swapped(above) + swapped(below)
    with jax.named_scope("solve"):
        rows, lists = kernel_call(
            solve_kernel,
            (sds((2 * BLK, ORDER), f32), sds((2 * SLAB // CHUNK, 128), jnp.int32)),
            (sub_blocks, sub_count, order) + window,
            [SMEM] * 3 + [VMEM] * 24,
            scratch=[
                pltpu.SMEM((2, 3 * 16), jnp.int32),
                pltpu.VMEM((2, ORDER + BLK, 3 * SLAB), f32),
                pltpu.VMEM((3 * SLAB, ORDER), f32),
                pltpu.VMEM((2, ORDER, ORDER), f32),
                pltpu.VMEM((8, ORDER), jnp.int32),
            ],
            limit=24,
            flops=12 * ORDER**3,
            moved=8 << 20,
        )
    with jax.named_scope("share"):
        rows = shared(rows)
    with jax.named_scope("half_back"):
        own, up, down = kernel_call(
            back_kernel,
            parts,
            (lists, places) + rows + (win_hi, win_lo, mask),
            [SMEM, SMEM] + [VMEM] * 11,
            scratch=[
                pltpu.VMEM((SLAB, ORDER), f32),
                pltpu.VMEM((SLAB, LANES), f32),
                pltpu.VMEM((4, ORDER, LANES), bf16),
                pltpu.VMEM((4, ORDER, LANES), bf16),
            ],
            **product,
        )
        above, below = passed_along(up, "rows", 1), passed_along(down, "rows", -1)
    with jax.named_scope("density"):
        packed = kernel_call(
            density_kernel,
            sds((SLAB // CHUNK, 3 * CHUNK // 2, 2 * CHUNK), f32),
            (root_hi, root_lo, above, own, below, mask),
            [VMEM] * 6,
            **product,
        )
        packed = lax.all_to_all(packed, ALL, 0, 0)
        density, charges = kernel_call(
            final_kernel,
            (sds((CHUNK, 3 * SLAB), f32), sds((1, CHUNK), f32)),
            (packed,),
            [VMEM],
            flops=1 << 20,
            moved=1 << 20,
        )
    return density, charges.reshape(CHUNK)


def solution(mesh):
    return jax.shard_map(
        shards,
        mesh=mesh,
        in_specs=(
            P(("rows", "cols", "space"), None),
            P("rows", None),
            P(),
            P(("rows", "cols", "space"), None),
            P(("rows", "cols", "space")),
        ),
        out_specs=(P(("rows", "cols", "space"), None), P(("rows", "cols", "space"))),
        check_vma=False,
    )
```

```python
import functools

import jax
import jax.numpy as jnp
from jax import lax
from jax.experimental import pallas as pl
from jax.experimental.pallas import tpu as pltpu
from jax.sharding import PartitionSpec as P

BLK = 32
MAXB = 16
SLAB = 512
CHUNK = 64
LANES = 256
ORDER = MAXB * BLK
f32 = jnp.float32
bf16 = jnp.bfloat16
ALL = ("cols", "space")
VMEM = pl.BlockSpec(memory_space=pltpu.VMEM)
SMEM = pl.BlockSpec(memory_space=pltpu.SMEM)


def passed_along(value, axis, steps):
    count = lax.axis_size(axis)
    pairs = [(source, (source + steps) % count) for source in range(count)]
    return lax.ppermute(value, axis, pairs)


def around(value):
    return value, passed_along(value, "cols", 1), passed_along(value, "cols", -1)


def swapped(values):
    return values + tuple(passed_along(value, "space", 1) for value in values)


def shared(value):
    return swapped(lax.optimization_barrier(around(value) + (passed_along(value, "cols", 2),)))


def kernel_call(body, shapes, operands, in_specs, scratch=(), limit=12, flops=0, moved=0):
    return pl.pallas_call(
        body,
        out_shape=shapes,
        in_specs=in_specs,
        out_specs=jax.tree.map(lambda _: VMEM, shapes),
        scratch_shapes=list(scratch),
        compiler_params=pltpu.CompilerParams(vmem_limit_bytes=limit << 20),
        cost_estimate=pl.CostEstimate(flops=flops, bytes_accessed=moved, transcendentals=0),
    )(*operands)


def split(x):
    high = x.astype(bf16)
    return high, (x - high.astype(f32)).astype(bf16)


def dot3(a, b):
    dot = functools.partial(jnp.dot, preferred_element_type=f32)
    return dot(a[0], b[0]) + (dot(a[0], b[1]) + dot(a[1], b[0]))


def send_parts(full, own, up, down):
    own[...] = full
    up[...] = pltpu.roll(full, LANES - CHUNK, 1)[:, : 2 * CHUNK]
    down[...] = full[:, : 2 * CHUNK]


def window_parts(above, own, below):
    blank = jnp.zeros((SLAB, 2 * CHUNK), f32)
    return (
        jnp.concatenate([above, blank], axis=1),
        own,
        pltpu.roll(jnp.concatenate([below, blank], axis=1), CHUNK, 1),
    )


def split_kernel(root, root_hi, root_lo):
    root_hi[...], root_lo[...] = split(root[...])


def first_kernel(order, *refs):
    pieces, refs = refs[:8], refs[8:]
    above, mine, below, mask, own, up, down, win_hi, win_lo, ham_hi, ham_lo = refs
    for k, part in enumerate(window_parts(above[...], mine[...], below[...])):
        cut = slice(k * SLAB, (k + 1) * SLAB)
        win_hi[cut, :], win_lo[cut, :] = split(part)
    for n, piece in enumerate(pieces):
        there = pl.ds(pl.multiple_of(order[n] * CHUNK, CHUNK), CHUNK)
        ham_hi[there, :], ham_lo[there, :] = split(piece[...])
    total = jnp.zeros((SLAB, LANES), f32)
    for k in range(3):
        cut = slice(k * SLAB, (k + 1) * SLAB)
        total += dot3((ham_hi[:, cut], ham_lo[:, cut]), (win_hi[cut, :], win_lo[cut, :]))
    send_parts(total * mask[...], own, up, down)


def root_product(root_hi, root_lo, above, own, below, mask):
    total = jnp.zeros((SLAB, LANES), f32)
    for k, part in enumerate(window_parts(above[...], own[...], below[...])):
        cut = slice(k * SLAB, (k + 1) * SLAB)
        total += dot3((root_hi[:, cut], root_lo[:, cut]), split(part))
    return total * mask[...]


def ortho_kernel(blocks, root_hi, root_lo, above, own, below, mask, mine, up, down):
    turned = root_product(root_hi, root_lo, above, own, below, mask).T
    mine[: 3 * CHUNK, :] = turned[: 3 * CHUNK]
    line = lax.broadcasted_iota(jnp.int32, (8, SLAB), 0)
    lane = lax.broadcasted_iota(jnp.int32, (8, SLAB), 1)
    lists = jnp.zeros((8, SLAB), jnp.int32)
    for g in range(2):
        for i in range(MAXB):
            lists = jnp.where((line == g) & (lane == i), blocks[g, i], lists)
    mine[3 * CHUNK :, :] = lists.astype(f32)
    up[...] = turned[CHUNK : 3 * CHUNK]
    down[...] = turned[: 2 * CHUNK]


def density_kernel(root_hi, root_lo, above, own, below, mask, packed):
    full = root_product(root_hi, root_lo, above, own, below, mask)
    half = CHUNK // 2
    for c in range(SLAB // CHUNK):
        rows = full[c * CHUNK : (c + 1) * CHUNK]
        packed[c, :CHUNK, :] = rows[:, : 2 * CHUNK]
        last = rows[:, 2 * CHUNK :]
        lane = lax.broadcasted_iota(jnp.int32, (half, 2 * CHUNK), 1)
        packed[c, CHUNK:, :] = jnp.where(lane < CHUNK, last[:half], pltpu.roll(last[half:], CHUNK, 1))


def solve_kernel(blocks, counts, order, *refs):
    pieces, (out, lists, inverse, rows, turned, assembled, valid) = refs[:24], refs[24:]
    row_id = lax.broadcasted_iota(jnp.int32, (BLK, ORDER), 0)
    col_id = lax.broadcasted_iota(jnp.int32, (BLK, ORDER), 1)
    list_id = lax.broadcasted_iota(jnp.int32, (1, ORDER), 1) // BLK
    dot = functools.partial(jnp.dot, preferred_element_type=f32)

    for g in range(2):
        for q in range(3 * 16):
            inverse[g, q] = MAXB
        for k in range(MAXB):
            inverse[g, blocks[g, k]] = k
    for n in range(8):
        lists[2 * n : 2 * n + 2, :] = pieces[n][3 * CHUNK : 3 * CHUNK + 2, :128].astype(jnp.int32)
        for panel, piece, first in ((1, pieces[n], 0), (0, pieces[8 + n], 0), (2, pieces[16 + n], 1)):
            for at in range(6 if panel == 1 else 4):
                q = (first + at // 2) * 16 + 2 * order[n] + at % 2
                block = piece[at * BLK : (at + 1) * BLK, :]
                for g in range(2):
                    there = pl.ds(pl.multiple_of(inverse[g, q] * BLK, BLK), BLK)
                    rows[g, there, panel * SLAB : (panel + 1) * SLAB] = block

    def gather(g):
        for panel in range(3):
            flags = jnp.zeros((1, ORDER), jnp.int32)
            for k in range(MAXB):
                keep = (k < counts[g]) & (jnp.abs(blocks[g, k] // 16 - panel) <= 1)
                flags = jnp.where(list_id == k, jnp.where(keep, 1, 0), flags)
            valid[panel : panel + 1, :] = flags
            cut = slice(panel * SLAB, (panel + 1) * SLAB)
            turned[cut, :] = rows[g, :ORDER, cut].T

        def one_column(k, carry):
            p = blocks[g, k]
            there = pl.ds(pl.multiple_of(k * BLK, BLK), BLK)
            source = pl.ds(pl.multiple_of(p * BLK, BLK), BLK)
            keep = valid[pl.ds(p // 16, 1), :] + jnp.where(k < counts[g], 0, -1) > 0
            assembled[g, there, :] = jnp.where(keep, turned[source, :], 0.0)
            return carry

        lax.fori_loop(0, MAXB, one_column, 0, unroll=4)

    def scaled(g):
        whole_block = assembled[g]
        symmetric = 0.5 * (whole_block + whole_block.T)
        squares = jnp.sum(symmetric * symmetric, keepdims=True) + 1e-06
        size = jnp.full((1, 1), counts[g] * BLK, jnp.int32).astype(f32)
        return symmetric * (jnp.sqrt(size) / (2.0 * jnp.sqrt(squares)))

    def step(iterate):
        parts = split(iterate)
        return 1.5 * iterate - 0.5 * dot3(parts, split(dot3(parts, parts)))

    def thin(home, parts):
        high, low = split(home)
        both = dot(jnp.concatenate([high, low], axis=0), parts[0])
        return both[:BLK] + both[BLK:] + dot(high, parts[1])

    for g in range(2):
        gather(g)
    iterates = [step(iterate) for iterate in [scaled(g) for g in range(2)]]
    for g, iterate in enumerate(iterates):
        parts = split(iterate)
        home = iterate[:BLK]
        home = 1.5 * home - 0.5 * thin(thin(home, parts), parts)
        out[g * BLK : (g + 1) * BLK, :] = 0.5 * (jnp.where(row_id == col_id, 1.0, 0.0) - home)


def back_kernel(blocks, places, *refs):
    pieces, (win_hi, win_lo, mask, own, up, down, rows, full, part_hi, part_lo) = refs[:8], refs[8:]
    for n, piece in enumerate(pieces):
        rows[n * 2 * BLK : (n + 1) * 2 * BLK, :] = piece[...]
    dot = functools.partial(jnp.dot, preferred_element_type=f32)
    width = part_hi.shape[0]

    def some_blocks(step, carry):
        for slot in range(width):
            e = step * width + slot
            g = places[e]
            for i in range(MAXB):
                source = pl.ds(pl.multiple_of(blocks[e, i] * BLK, BLK), BLK)
                target = slice(i * BLK, (i + 1) * BLK)
                part_hi[slot, target, :] = win_hi[source, :]
                part_lo[slot, target, :] = win_lo[source, :]
            high, low = split(rows[pl.ds(pl.multiple_of(e * BLK, BLK), BLK), :])
            both = dot(jnp.concatenate([high, low], axis=0), part_hi[slot])
            there = pl.ds(pl.multiple_of(g * BLK, BLK), BLK)
            total = both[:BLK] + both[BLK:] + dot(high, part_lo[slot])
            full[there, :] = total * mask[there, :]
        return carry

    lax.fori_loop(0, SLAB // BLK // width, some_blocks, 0)
    send_parts(full[...], own, up, down)


def final_kernel(packed, density, charges):
    half = CHUNK // 2
    first = lax.broadcasted_iota(jnp.int32, (CHUNK, 128), 1) < CHUNK
    total = jnp.zeros((CHUNK, 128), f32)
    for m in range(SLAB // (2 * CHUNK)):
        a, b = packed[2 * m], packed[2 * m + 1]
        ab, bb = a[:CHUNK], b[:CHUNK]
        a2, b2 = a[CHUNK:], b[CHUNK:]
        left = jnp.where(first, ab, pltpu.roll(bb, CHUNK, 1))
        middle = jnp.where(first, pltpu.roll(ab, CHUNK, 1), bb)
        right = jnp.concatenate(
            [
                jnp.where(first[:half], a2, pltpu.roll(b2, CHUNK, 1)),
                jnp.where(first[:half], pltpu.roll(a2, CHUNK, 1), b2),
            ],
            axis=0,
        )
        for j, part in enumerate((left, middle, right)):
            density[:, j * SLAB + m * 128 : j * SLAB + (m + 1) * 128] = part
        total += left + middle + right
    charges[...] = jnp.sum(total.T, axis=0, keepdims=True)


def shards(hamiltonian, root, pattern, sub_blocks, sub_count):
    sds = jax.ShapeDtypeStruct
    slab = lax.axis_index("rows")
    col, core = lax.axis_index("cols"), lax.axis_index("space")
    home = 2 * col + core
    parts = (sds((SLAB, LANES), f32), sds((SLAB, 2 * CHUNK), f32), sds((SLAB, 2 * CHUNK), f32))
    product = dict(flops=6 * SLAB * 3 * SLAB * LANES, moved=6 << 20)

    with jax.named_scope("inputs"):
        chips = jnp.stack([col, (col + 3) % 4, (col + 1) % 4, (col + 2) % 4])
        order = jnp.concatenate([2 * chips + core, 2 * chips + 1 - core]).astype(jnp.int32)
        places = (2 * order[:, None] + jnp.arange(2, dtype=jnp.int32)[None, :]).reshape(-1)
        pieces = [lax.dynamic_slice(root, (0, j * SLAB + home * CHUNK), (SLAB, CHUNK)) for j in range(3)]
        above = passed_along(jnp.concatenate(pieces[1:], axis=1), "rows", 1)
        below = passed_along(jnp.concatenate(pieces[:2], axis=1), "rows", -1)
        ham = around(hamiltonian) + (passed_along(hamiltonian, "cols", 2),)
        own = jnp.concatenate(pieces + [jnp.zeros((SLAB, CHUNK), f32)], axis=1)
        mask = lax.dynamic_slice(pattern, (slab * 16, 0), (16, 48)).astype(f32).reshape(16, 3, 16)
        mask = lax.dynamic_slice(mask, (0, 0, 2 * home), (16, 3, 2)).reshape(16, 6)
        mask = jnp.pad(mask, ((0, 0), (0, 2)))
        mask = jnp.broadcast_to(mask[:, None, :, None], (16, BLK, 8, BLK)).reshape(SLAB, LANES)
        root_hi, root_lo = kernel_call(
            split_kernel,
            (sds((SLAB, 3 * SLAB), bf16),) * 2,
            (root,),
            [VMEM],
            limit=8,
            flops=1 << 22,
            moved=8 << 20,
        )
        chips = jnp.stack([col, (col + 3) % 4, (col + 1) % 4, (col + 2) % 4])
        order = jnp.concatenate([2 * chips + core, 2 * chips + 1 - core]).astype(jnp.int32)
        places = (2 * order[:, None] + jnp.arange(2, dtype=jnp.int32)[None, :]).reshape(-1)
        ready = (above, below, own, mask, root_hi, root_lo, order, places, ham)
        above, below, own, mask, root_hi, root_lo, order, places, ham = lax.optimization_barrier(ready)
        ham = swapped(ham)
    with jax.named_scope("half_done"):
        own, up, down, win_hi, win_lo = kernel_call(
            first_kernel,
            parts + (sds((3 * SLAB, LANES), bf16),) * 2,
            (order,) + ham + (above, own, below, mask),
            [SMEM] + [VMEM] * 12,
            scratch=[pltpu.VMEM((SLAB, 3 * SLAB), bf16)] * 2,
            limit=16,
            **product,
        )
        above, below = passed_along(up, "rows", 1), passed_along(down, "rows", -1)
    with jax.named_scope("orthogonal"):
        mine, up, down = kernel_call(
            ortho_kernel,
            (sds((3 * CHUNK + 8, SLAB), f32),) + (sds((2 * CHUNK, SLAB), f32),) * 2,
            (sub_blocks, root_hi, root_lo, above, own, below, mask),
            [SMEM] + [VMEM] * 6,
            **product,
        )
        above, below = passed_along(up, "rows", 1), passed_along(down, "rows", -1)
        _, before, after = around(mine)
        far = passed_along(mine, "cols", 2)
        above = around(above)
        below, *above = lax.optimization_barrier((below,) + above)
        below = around(below)
        above = tuple(above)
        above += (passed_along(far[CHUNK : 3 * CHUNK], "rows", 1),)
        below += (passed_along(far[: 2 * CHUNK], "rows", -1),)
        whole, above = lax.optimization_barrier(((mine, before, after, far), above))
        below = lax.optimization_barrier(below)
        window = swapped(whole) + swapped(above) + swapped(below)
    with jax.named_scope("solve"):
        rows, lists = kernel_call(
            solve_kernel,
            (sds((2 * BLK, ORDER), f32), sds((2 * SLAB // CHUNK, 128), jnp.int32)),
            (sub_blocks, sub_count, order) + window,
            [SMEM] * 3 + [VMEM] * 24,
            scratch=[
                pltpu.SMEM((2, 3 * 16), jnp.int32),
                pltpu.VMEM((2, ORDER + BLK, 3 * SLAB), f32),
                pltpu.VMEM((3 * SLAB, ORDER), f32),
                pltpu.VMEM((2, ORDER, ORDER), f32),
                pltpu.VMEM((8, ORDER), jnp.int32),
            ],
            limit=24,
            flops=12 * ORDER**3,
            moved=8 << 20,
        )
    with jax.named_scope("share"):
        rows = shared(rows)
    with jax.named_scope("half_back"):
        own, up, down = kernel_call(
            back_kernel,
            parts,
            (lists, places) + rows + (win_hi, win_lo, mask),
            [SMEM, SMEM] + [VMEM] * 11,
            scratch=[
                pltpu.VMEM((SLAB, ORDER), f32),
                pltpu.VMEM((SLAB, LANES), f32),
                pltpu.VMEM((4, ORDER, LANES), bf16),
                pltpu.VMEM((4, ORDER, LANES), bf16),
            ],
            **product,
        )
        above, below = passed_along(up, "rows", 1), passed_along(down, "rows", -1)
    with jax.named_scope("density"):
        packed = kernel_call(
            density_kernel,
            sds((SLAB // CHUNK, 3 * CHUNK // 2, 2 * CHUNK), f32),
            (root_hi, root_lo, above, own, below, mask),
            [VMEM] * 6,
            **product,
        )
        packed = lax.all_to_all(packed, ALL, 0, 0)
        density, charges = kernel_call(
            final_kernel,
            (sds((CHUNK, 3 * SLAB), f32), sds((1, CHUNK), f32)),
            (packed,),
            [VMEM],
            flops=1 << 20,
            moved=1 << 20,
        )
    return density, charges.reshape(CHUNK)


def solution(mesh):
    return jax.shard_map(
        shards,
        mesh=mesh,
        in_specs=(
            P(("rows", "cols", "space"), None),
            P("rows", None),
            P(),
            P(("rows", "cols", "space"), None),
            P(("rows", "cols", "space")),
        ),
        out_specs=(P(("rows", "cols", "space"), None), P(("rows", "cols", "space"))),
        check_vma=False,
    )
```

```python
import functools

import jax
import jax.numpy as jnp
from jax import lax
from jax.experimental import pallas as pl
from jax.experimental.pallas import tpu as pltpu
from jax.sharding import PartitionSpec as P

BLK = 32
MAXB = 16
SLAB = 512
CHUNK = 64
LANES = 256
ORDER = MAXB * BLK
f32 = jnp.float32
bf16 = jnp.bfloat16
ALL = ("cols", "space")
VMEM = pl.BlockSpec(memory_space=pltpu.VMEM)
SMEM = pl.BlockSpec(memory_space=pltpu.SMEM)


def passed_along(value, axis, steps):
    count = lax.axis_size(axis)
    pairs = [(source, (source + steps) % count) for source in range(count)]
    return lax.ppermute(value, axis, pairs)


def around(value):
    return value, passed_along(value, "cols", 1), passed_along(value, "cols", -1)


def swapped(values):
    return values + tuple(passed_along(value, "space", 1) for value in values)


def shared(value):
    return swapped(around(value) + (passed_along(value, "cols", 2),))


def kernel_call(body, shapes, operands, in_specs, scratch=(), limit=12, flops=0, moved=0):
    return pl.pallas_call(
        body,
        out_shape=shapes,
        in_specs=in_specs,
        out_specs=jax.tree.map(lambda _: VMEM, shapes),
        scratch_shapes=list(scratch),
        compiler_params=pltpu.CompilerParams(vmem_limit_bytes=limit << 20),
        cost_estimate=pl.CostEstimate(flops=flops, bytes_accessed=moved, transcendentals=0),
    )(*operands)


def split(x):
    high = x.astype(bf16)
    return high, (x - high.astype(f32)).astype(bf16)


def dot3(a, b):
    dot = functools.partial(jnp.dot, preferred_element_type=f32)
    return dot(a[0], b[0]) + (dot(a[0], b[1]) + dot(a[1], b[0]))


def send_parts(full, own, up, down):
    own[...] = full
    up[...] = pltpu.roll(full, LANES - CHUNK, 1)[:, : 2 * CHUNK]
    down[...] = full[:, : 2 * CHUNK]


def window_parts(above, own, below):
    blank = jnp.zeros((SLAB, 2 * CHUNK), f32)
    return (
        jnp.concatenate([above, blank], axis=1),
        own,
        pltpu.roll(jnp.concatenate([below, blank], axis=1), CHUNK, 1),
    )


def split_kernel(root, root_hi, root_lo):
    root_hi[...], root_lo[...] = split(root[...])


def first_kernel(order, *refs):
    pieces, refs = refs[:8], refs[8:]
    above, mine, below, mask, own, up, down, win_hi, win_lo, ham_hi, ham_lo = refs
    for k, part in enumerate(window_parts(above[...], mine[...], below[...])):
        cut = slice(k * SLAB, (k + 1) * SLAB)
        win_hi[cut, :], win_lo[cut, :] = split(part)
    for n, piece in enumerate(pieces):
        there = pl.ds(pl.multiple_of(order[n] * CHUNK, CHUNK), CHUNK)
        ham_hi[there, :], ham_lo[there, :] = split(piece[...])
    total = jnp.zeros((SLAB, LANES), f32)
    for k in range(3):
        cut = slice(k * SLAB, (k + 1) * SLAB)
        total += dot3((ham_hi[:, cut], ham_lo[:, cut]), (win_hi[cut, :], win_lo[cut, :]))
    send_parts(total * mask[...], own, up, down)


def root_product(root_hi, root_lo, above, own, below, mask):
    total = jnp.zeros((SLAB, LANES), f32)
    for k, part in enumerate(window_parts(above[...], own[...], below[...])):
        cut = slice(k * SLAB, (k + 1) * SLAB)
        total += dot3((root_hi[:, cut], root_lo[:, cut]), split(part))
    return total * mask[...]


def ortho_kernel(blocks, root_hi, root_lo, above, own, below, mask, mine, up, down):
    turned = root_product(root_hi, root_lo, above, own, below, mask).T
    mine[: 3 * CHUNK, :] = turned[: 3 * CHUNK]
    up[...] = turned[CHUNK : 3 * CHUNK]
    down[...] = turned[: 2 * CHUNK]
    line = lax.broadcasted_iota(jnp.int32, (8, SLAB), 0)
    lane = lax.broadcasted_iota(jnp.int32, (8, SLAB), 1)
    lists = jnp.zeros((8, SLAB), jnp.int32)
    for g in range(2):
        for i in range(MAXB):
            lists = jnp.where((line == g) & (lane == i), blocks[g, i], lists)
    mine[3 * CHUNK :, :] = lists.astype(f32)


def density_kernel(root_hi, root_lo, above, own, below, mask, packed):
    full = root_product(root_hi, root_lo, above, own, below, mask)
    half = CHUNK // 2
    for c in range(SLAB // CHUNK):
        rows = full[c * CHUNK : (c + 1) * CHUNK]
        packed[c, :CHUNK, :] = rows[:, : 2 * CHUNK]
        last = rows[:, 2 * CHUNK :]
        lane = lax.broadcasted_iota(jnp.int32, (half, 2 * CHUNK), 1)
        packed[c, CHUNK:, :] = jnp.where(lane < CHUNK, last[:half], pltpu.roll(last[half:], CHUNK, 1))


def solve_kernel(blocks, counts, order, *refs):
    pieces, (out, lists, inverse, rows, turned, assembled, valid) = refs[:24], refs[24:]
    row_id = lax.broadcasted_iota(jnp.int32, (BLK, ORDER), 0)
    col_id = lax.broadcasted_iota(jnp.int32, (BLK, ORDER), 1)
    list_id = lax.broadcasted_iota(jnp.int32, (1, ORDER), 1) // BLK
    dot = functools.partial(jnp.dot, preferred_element_type=f32)

    for g in range(2):
        for q in range(3 * 16):
            inverse[g, q] = MAXB
        for k in range(MAXB):
            inverse[g, blocks[g, k]] = k
    for n in range(8):
        lists[2 * n : 2 * n + 2, :] = pieces[n][3 * CHUNK : 3 * CHUNK + 2, :128].astype(jnp.int32)
        for panel, piece, first in ((1, pieces[n], 0), (0, pieces[8 + n], 0), (2, pieces[16 + n], 1)):
            for at in range(6 if panel == 1 else 4):
                q = (first + at // 2) * 16 + 2 * order[n] + at % 2
                block = piece[at * BLK : (at + 1) * BLK, :]
                for g in range(2):
                    there = pl.ds(pl.multiple_of(inverse[g, q] * BLK, BLK), BLK)
                    rows[g, there, panel * SLAB : (panel + 1) * SLAB] = block

    def gather(g):
        for panel in range(3):
            flags = jnp.zeros((1, ORDER), jnp.int32)
            for k in range(MAXB):
                keep = (k < counts[g]) & (jnp.abs(blocks[g, k] // 16 - panel) <= 1)
                flags = jnp.where(list_id == k, jnp.where(keep, 1, 0), flags)
            valid[panel : panel + 1, :] = flags
            cut = slice(panel * SLAB, (panel + 1) * SLAB)
            turned[cut, :] = rows[g, :ORDER, cut].T

        def one_column(k, carry):
            p = blocks[g, k]
            there = pl.ds(pl.multiple_of(k * BLK, BLK), BLK)
            source = pl.ds(pl.multiple_of(p * BLK, BLK), BLK)
            keep = valid[pl.ds(p // 16, 1), :] + jnp.where(k < counts[g], 0, -1) > 0
            assembled[g, there, :] = jnp.where(keep, turned[source, :], 0.0)
            return carry

        lax.fori_loop(0, MAXB, one_column, 0, unroll=4)

    def scaled(g):
        whole_block = assembled[g]
        symmetric = 0.5 * (whole_block + whole_block.T)
        squares = jnp.sum(symmetric * symmetric, keepdims=True) + 1e-06
        size = jnp.full((1, 1), counts[g] * BLK, jnp.int32).astype(f32)
        return symmetric * (jnp.sqrt(size) / (2.0 * jnp.sqrt(squares)))

    def thin(home, parts):
        high, low = split(home)
        both = dot(jnp.concatenate([high, low], axis=0), parts[0])
        return both[:BLK] + both[BLK:] + dot(high, parts[1])

    for g in range(2):
        gather(g)
    iterates = [scaled(g) for g in range(2)]
    squares = [split(dot3(parts, parts)) for parts in [split(iterate) for iterate in iterates]]
    firsts = [iterate[:BLK] for iterate in iterates]
    firsts = [1.5 * first - 0.5 * thin(first, square) for first, square in zip(firsts, squares)]
    cubes = [thin(first, square) for first, square in zip(firsts, squares)]
    for _ in range(2):
        cubes = [1.5 * cube - 0.5 * thin(cube, square) for cube, square in zip(cubes, squares)]
    for g in range(2):
        home = 1.5 * firsts[g] - 0.5 * cubes[g]
        out[g * BLK : (g + 1) * BLK, :] = 0.5 * (jnp.where(row_id == col_id, 1.0, 0.0) - home)


def back_kernel(blocks, places, *refs):
    pieces, (win_hi, win_lo, mask, own, up, down, rows, full, part_hi, part_lo) = refs[:8], refs[8:]
    for n, piece in enumerate(pieces):
        rows[n * 2 * BLK : (n + 1) * 2 * BLK, :] = piece[...]
    dot = functools.partial(jnp.dot, preferred_element_type=f32)
    width = part_hi.shape[0]

    def some_blocks(step, carry):
        for slot in range(width):
            e = step * width + slot
            g = places[e]
            for i in range(MAXB):
                source = pl.ds(pl.multiple_of(blocks[e, i] * BLK, BLK), BLK)
                target = slice(i * BLK, (i + 1) * BLK)
                part_hi[slot, target, :] = win_hi[source, :]
                part_lo[slot, target, :] = win_lo[source, :]
            high, low = split(rows[pl.ds(pl.multiple_of(e * BLK, BLK), BLK), :])
            both = dot(jnp.concatenate([high, low], axis=0), part_hi[slot])
            there = pl.ds(pl.multiple_of(g * BLK, BLK), BLK)
            total = both[:BLK] + both[BLK:] + dot(high, part_lo[slot])
            full[there, :] = total * mask[there, :]
        return carry

    lax.fori_loop(0, SLAB // BLK // width, some_blocks, 0)
    send_parts(full[...], own, up, down)


def final_kernel(packed, density, charges):
    half = CHUNK // 2
    first = lax.broadcasted_iota(jnp.int32, (CHUNK, 128), 1) < CHUNK
    total = jnp.zeros((CHUNK, 128), f32)
    for m in range(SLAB // (2 * CHUNK)):
        a, b = packed[2 * m], packed[2 * m + 1]
        ab, bb = a[:CHUNK], b[:CHUNK]
        a2, b2 = a[CHUNK:], b[CHUNK:]
        left = jnp.where(first, ab, pltpu.roll(bb, CHUNK, 1))
        middle = jnp.where(first, pltpu.roll(ab, CHUNK, 1), bb)
        right = jnp.concatenate(
            [
                jnp.where(first[:half], a2, pltpu.roll(b2, CHUNK, 1)),
                jnp.where(first[:half], pltpu.roll(a2, CHUNK, 1), b2),
            ],
            axis=0,
        )
        for j, part in enumerate((left, middle, right)):
            density[:, j * SLAB + m * 128 : j * SLAB + (m + 1) * 128] = part
        total += left + middle + right
    charges[...] = jnp.sum(total.T, axis=0, keepdims=True)


def shards(hamiltonian, root, pattern, sub_blocks, sub_count):
    sds = jax.ShapeDtypeStruct
    slab = lax.axis_index("rows")
    col, core = lax.axis_index("cols"), lax.axis_index("space")
    home = 2 * col + core
    parts = (sds((SLAB, LANES), f32), sds((SLAB, 2 * CHUNK), f32), sds((SLAB, 2 * CHUNK), f32))
    product = dict(flops=6 * SLAB * 3 * SLAB * LANES, moved=6 << 20)

    with jax.named_scope("inputs"):
        chips = jnp.stack([col, (col + 3) % 4, (col + 1) % 4, (col + 2) % 4])
        order = jnp.concatenate([2 * chips + core, 2 * chips + 1 - core]).astype(jnp.int32)
        places = (2 * order[:, None] + jnp.arange(2, dtype=jnp.int32)[None, :]).reshape(-1)
        pieces = [lax.dynamic_slice(root, (0, j * SLAB + home * CHUNK), (SLAB, CHUNK)) for j in range(3)]
        above = passed_along(jnp.concatenate(pieces[1:], axis=1), "rows", 1)
        below = passed_along(jnp.concatenate(pieces[:2], axis=1), "rows", -1)
        ham = around(hamiltonian) + (passed_along(hamiltonian, "cols", 2),)
        own = jnp.concatenate(pieces + [jnp.zeros((SLAB, CHUNK), f32)], axis=1)
        mask = lax.dynamic_slice(pattern, (slab * 16, 0), (16, 48)).astype(f32).reshape(16, 3, 16)
        mask = lax.dynamic_slice(mask, (0, 0, 2 * home), (16, 3, 2)).reshape(16, 6)
        mask = jnp.pad(mask, ((0, 0), (0, 2)))
        mask = jnp.broadcast_to(mask[:, None, :, None], (16, BLK, 8, BLK)).reshape(SLAB, LANES)
        root_hi, root_lo = kernel_call(
            split_kernel,
            (sds((SLAB, 3 * SLAB), bf16),) * 2,
            (root,),
            [VMEM],
            limit=8,
            flops=1 << 22,
            moved=8 << 20,
        )
        chips = jnp.stack([col, (col + 3) % 4, (col + 1) % 4, (col + 2) % 4])
        order = jnp.concatenate([2 * chips + core, 2 * chips + 1 - core]).astype(jnp.int32)
        places = (2 * order[:, None] + jnp.arange(2, dtype=jnp.int32)[None, :]).reshape(-1)
        ready = (above, below, own, mask, root_hi, root_lo, order, places, ham)
        above, below, own, mask, root_hi, root_lo, order, places, ham = lax.optimization_barrier(ready)
        ham = swapped(ham)
    with jax.named_scope("half_done"):
        own, up, down, win_hi, win_lo = kernel_call(
            first_kernel,
            parts + (sds((3 * SLAB, LANES), bf16),) * 2,
            (order,) + ham + (above, own, below, mask),
            [SMEM] + [VMEM] * 12,
            scratch=[pltpu.VMEM((SLAB, 3 * SLAB), bf16)] * 2,
            limit=16,
            **product,
        )
        above, below = passed_along(up, "rows", 1), passed_along(down, "rows", -1)
    with jax.named_scope("orthogonal"):
        mine, up, down = kernel_call(
            ortho_kernel,
            (sds((3 * CHUNK + 8, SLAB), f32),) + (sds((2 * CHUNK, SLAB), f32),) * 2,
            (sub_blocks, root_hi, root_lo, above, own, below, mask),
            [SMEM] + [VMEM] * 6,
            **product,
        )
        above, below = passed_along(up, "rows", 1), passed_along(down, "rows", -1)
        _, before, after = around(mine)
        far = passed_along(mine, "cols", 2)
        above, before = lax.optimization_barrier((above, before))
        below, after = lax.optimization_barrier((below, after))
        above = around(above) + (passed_along(far[CHUNK : 3 * CHUNK], "rows", 1),)
        below = around(below) + (passed_along(below, "cols", 2),)
        whole, above = lax.optimization_barrier(((mine, before, after, far), above))
        below = lax.optimization_barrier(below)
        window = swapped(whole) + swapped(above) + swapped(below)
    with jax.named_scope("solve"):
        rows, lists = kernel_call(
            solve_kernel,
            (sds((2 * BLK, ORDER), f32), sds((2 * SLAB // CHUNK, 128), jnp.int32)),
            (sub_blocks, sub_count, order) + window,
            [SMEM] * 3 + [VMEM] * 24,
            scratch=[
                pltpu.SMEM((2, 3 * 16), jnp.int32),
                pltpu.VMEM((2, ORDER + BLK, 3 * SLAB), f32),
                pltpu.VMEM((3 * SLAB, ORDER), f32),
                pltpu.VMEM((2, ORDER, ORDER), f32),
                pltpu.VMEM((8, ORDER), jnp.int32),
            ],
            limit=24,
            flops=12 * ORDER**3,
            moved=8 << 20,
        )
    with jax.named_scope("share"):
        rows = shared(rows)
    with jax.named_scope("half_back"):
        own, up, down = kernel_call(
            back_kernel,
            parts,
            (lists, places) + rows + (win_hi, win_lo, mask),
            [SMEM, SMEM] + [VMEM] * 11,
            scratch=[
                pltpu.VMEM((SLAB, ORDER), f32),
                pltpu.VMEM((SLAB, LANES), f32),
                pltpu.VMEM((4, ORDER, LANES), bf16),
                pltpu.VMEM((4, ORDER, LANES), bf16),
            ],
            **product,
        )
        above, below = passed_along(up, "rows", 1), passed_along(down, "rows", -1)
    with jax.named_scope("density"):
        packed = kernel_call(
            density_kernel,
            sds((SLAB // CHUNK, 3 * CHUNK // 2, 2 * CHUNK), f32),
            (root_hi, root_lo, above, own, below, mask),
            [VMEM] * 6,
            **product,
        )
        packed = lax.all_to_all(packed, ALL, 0, 0)
        density, charges = kernel_call(
            final_kernel,
            (sds((CHUNK, 3 * SLAB), f32), sds((1, CHUNK), f32)),
            (packed,),
            [VMEM],
            flops=1 << 20,
            moved=1 << 20,
        )
    return density, charges.reshape(CHUNK)


def solution(mesh):
    return jax.shard_map(
        shards,
        mesh=mesh,
        in_specs=(
            P(("rows", "cols", "space"), None),
            P("rows", None),
            P(),
            P(("rows", "cols", "space"), None),
            P(("rows", "cols", "space")),
        ),
        out_specs=(P(("rows", "cols", "space"), None), P(("rows", "cols", "space"))),
        check_vma=False,
    )
```

```python
import functools

import jax
import jax.numpy as jnp
from jax import lax
from jax.experimental import pallas as pl
from jax.experimental.pallas import tpu as pltpu
from jax.sharding import PartitionSpec as P

BLK = 32
MAXB = 16
SLAB = 512
CHUNK = 64
LANES = 256
ORDER = MAXB * BLK
f32 = jnp.float32
bf16 = jnp.bfloat16
ALL = ("cols", "space")
VMEM = pl.BlockSpec(memory_space=pltpu.VMEM)
SMEM = pl.BlockSpec(memory_space=pltpu.SMEM)


def passed_along(value, axis, steps):
    count = lax.axis_size(axis)
    pairs = [(source, (source + steps) % count) for source in range(count)]
    return lax.ppermute(value, axis, pairs)


def met(value):
    return lax.ppermute(value, "rows", [(slab, slab ^ 1) for slab in range(lax.axis_size("rows"))])


def met_after(value):
    count = lax.axis_size("rows")
    return lax.ppermute(value, "rows", [(slab, (((slab - 1) ^ 1) + 1) % count) for slab in range(count)])


def around(value):
    return value, passed_along(value, "cols", 1), passed_along(value, "cols", -1)


def swapped(values):
    return values + tuple(passed_along(value, "space", 1) for value in values)


def shared(value):
    return swapped(around(value) + (passed_along(value, "cols", 2),))


def kernel_call(body, shapes, operands, in_specs, scratch=(), limit=12, flops=0, moved=0):
    return pl.pallas_call(
        body,
        out_shape=shapes,
        in_specs=in_specs,
        out_specs=jax.tree.map(lambda _: VMEM, shapes),
        scratch_shapes=list(scratch),
        compiler_params=pltpu.CompilerParams(vmem_limit_bytes=limit << 20),
        cost_estimate=pl.CostEstimate(flops=flops, bytes_accessed=moved, transcendentals=0),
    )(*operands)


def split(x):
    high = x.astype(bf16)
    return high, (x - high.astype(f32)).astype(bf16)


def dot3(a, b):
    dot = functools.partial(jnp.dot, preferred_element_type=f32)
    return dot(a[0], b[0]) + (dot(a[0], b[1]) + dot(a[1], b[0]))


def send_parts(full, odd, own, first, second):
    own[...] = full
    up = pltpu.roll(full, LANES - CHUNK, 1)[:, : 2 * CHUNK]
    down = full[:, : 2 * CHUNK]
    first[...] = jnp.where(odd, down, up)
    second[...] = jnp.where(odd, up, down)


def window_parts(first, own, second, odd):
    above, below = jnp.where(odd, first, second), jnp.where(odd, second, first)
    blank = jnp.zeros((SLAB, 2 * CHUNK), f32)
    return (
        jnp.concatenate([above, blank], axis=1),
        own,
        pltpu.roll(jnp.concatenate([below, blank], axis=1), CHUNK, 1),
    )


def split_kernel(root, root_hi, root_lo):
    root_hi[...], root_lo[...] = split(root[...])


def first_kernel(order, parity, *refs):
    odd = parity[0] == 1
    pieces, refs = refs[:8], refs[8:]
    above, mine, below, mask, own, up, down, win_hi, win_lo, ham_hi, ham_lo = refs
    for k, part in enumerate(window_parts(above[...], mine[...], below[...], True)):
        cut = slice(k * SLAB, (k + 1) * SLAB)
        win_hi[cut, :], win_lo[cut, :] = split(part)
    for n, piece in enumerate(pieces):
        there = pl.ds(pl.multiple_of(order[n] * CHUNK, CHUNK), CHUNK)
        ham_hi[there, :], ham_lo[there, :] = split(piece[...])
    total = jnp.zeros((SLAB, LANES), f32)
    for k in range(3):
        cut = slice(k * SLAB, (k + 1) * SLAB)
        total += dot3((ham_hi[:, cut], ham_lo[:, cut]), (win_hi[cut, :], win_lo[cut, :]))
    send_parts(total * mask[...], odd, own, up, down)


def root_product(odd, root_hi, root_lo, above, own, below, mask):
    total = jnp.zeros((SLAB, LANES), f32)
    for k, part in enumerate(window_parts(above[...], own[...], below[...], odd)):
        cut = slice(k * SLAB, (k + 1) * SLAB)
        total += dot3((root_hi[:, cut], root_lo[:, cut]), split(part))
    return total * mask[...]


def ortho_kernel(blocks, parity, root_hi, root_lo, above, own, below, mask, mine, first, second):
    odd = parity[0] == 1
    turned = root_product(odd, root_hi, root_lo, above, own, below, mask).T
    mine[: 3 * CHUNK, :] = turned[: 3 * CHUNK]
    up, down = turned[CHUNK : 3 * CHUNK], turned[: 2 * CHUNK]
    first[...] = jnp.where(odd, down, up)
    second[...] = jnp.where(odd, up, down)
    line = lax.broadcasted_iota(jnp.int32, (8, SLAB), 0)
    lane = lax.broadcasted_iota(jnp.int32, (8, SLAB), 1)
    lists = jnp.zeros((8, SLAB), jnp.int32)
    for g in range(2):
        for i in range(MAXB):
            lists = jnp.where((line == g) & (lane == i), blocks[g, i], lists)
    mine[3 * CHUNK :, :] = lists.astype(f32)


def density_kernel(parity, root_hi, root_lo, above, own, below, mask, packed):
    full = root_product(parity[0] == 1, root_hi, root_lo, above, own, below, mask)
    half = CHUNK // 2
    for c in range(SLAB // CHUNK):
        rows = full[c * CHUNK : (c + 1) * CHUNK]
        packed[c, :CHUNK, :] = rows[:, : 2 * CHUNK]
        last = rows[:, 2 * CHUNK :]
        lane = lax.broadcasted_iota(jnp.int32, (half, 2 * CHUNK), 1)
        packed[c, CHUNK:, :] = jnp.where(lane < CHUNK, last[:half], pltpu.roll(last[half:], CHUNK, 1))


def solve_kernel(blocks, counts, order, parity, *refs):
    pieces, (out, lists, inverse, rows, turned, assembled, valid) = refs[:24], refs[24:]
    row_id = lax.broadcasted_iota(jnp.int32, (BLK, ORDER), 0)
    col_id = lax.broadcasted_iota(jnp.int32, (BLK, ORDER), 1)
    list_id = lax.broadcasted_iota(jnp.int32, (1, ORDER), 1) // BLK
    dot = functools.partial(jnp.dot, preferred_element_type=f32)

    for g in range(2):
        for q in range(3 * 16):
            inverse[g, q] = MAXB
        for k in range(MAXB):
            inverse[g, blocks[g, k]] = k
    for n in range(8):
        lists[2 * n : 2 * n + 2, :] = pieces[n][3 * CHUNK : 3 * CHUNK + 2, :128].astype(jnp.int32)
        for piece, panel in ((pieces[n], 1), (pieces[8 + n], 2 - 2 * parity[0]), (pieces[16 + n], 2 * parity[0])):
            lanes = pl.ds(pl.multiple_of(panel * SLAB, SLAB), SLAB)
            for at in range(6 if piece is pieces[n] else 4):
                q = (panel // 2 + at // 2) * 16 + 2 * order[n] + at % 2
                block = piece[at * BLK : (at + 1) * BLK, :]
                for g in range(2):
                    there = pl.ds(pl.multiple_of(inverse[g, q] * BLK, BLK), BLK)
                    rows[g, there, lanes] = block

    def gather(g):
        for panel in range(3):
            flags = jnp.zeros((1, ORDER), jnp.int32)
            for k in range(MAXB):
                keep = (k < counts[g]) & (jnp.abs(blocks[g, k] // 16 - panel) <= 1)
                flags = jnp.where(list_id == k, jnp.where(keep, 1, 0), flags)
            valid[panel : panel + 1, :] = flags
            cut = slice(panel * SLAB, (panel + 1) * SLAB)
            turned[cut, :] = rows[g, :ORDER, cut].T

        def one_column(k, carry):
            p = blocks[g, k]
            there = pl.ds(pl.multiple_of(k * BLK, BLK), BLK)
            source = pl.ds(pl.multiple_of(p * BLK, BLK), BLK)
            keep = valid[pl.ds(p // 16, 1), :] + jnp.where(k < counts[g], 0, -1) > 0
            assembled[g, there, :] = jnp.where(keep, turned[source, :], 0.0)
            return carry

        lax.fori_loop(0, MAXB, one_column, 0, unroll=4)

    def scaled(g):
        whole_block = assembled[g]
        symmetric = 0.5 * (whole_block + whole_block.T)
        squares = jnp.sum(symmetric * symmetric, keepdims=True) + 1e-06
        size = jnp.full((1, 1), counts[g] * BLK, jnp.int32).astype(f32)
        return symmetric * (jnp.sqrt(size) / (2.0 * jnp.sqrt(squares)))

    def thin(home, parts):
        high, low = split(home)
        both = dot(jnp.concatenate([high, low], axis=0), parts[0])
        return both[:BLK] + both[BLK:] + dot(high, parts[1])

    for g in range(2):
        gather(g)
    iterates = [scaled(g) for g in range(2)]
    squares = [split(dot3(parts, parts)) for parts in [split(iterate) for iterate in iterates]]
    firsts = [iterate[:BLK] for iterate in iterates]
    firsts = [1.5 * first - 0.5 * thin(first, square) for first, square in zip(firsts, squares)]
    cubes = [thin(first, square) for first, square in zip(firsts, squares)]
    for _ in range(2):
        cubes = [1.5 * cube - 0.5 * thin(cube, square) for cube, square in zip(cubes, squares)]
    for g in range(2):
        home = 1.5 * firsts[g] - 0.5 * cubes[g]
        out[g * BLK : (g + 1) * BLK, :] = 0.5 * (jnp.where(row_id == col_id, 1.0, 0.0) - home)


def back_kernel(blocks, places, parity, *refs):
    pieces, (win_hi, win_lo, mask, own, up, down, rows, full, part_hi, part_lo) = refs[:8], refs[8:]
    for n, piece in enumerate(pieces):
        rows[n * 2 * BLK : (n + 1) * 2 * BLK, :] = piece[...]
    dot = functools.partial(jnp.dot, preferred_element_type=f32)
    width = part_hi.shape[0]

    def some_blocks(step, carry):
        for slot in range(width):
            e = step * width + slot
            g = places[e]
            for i in range(MAXB):
                source = pl.ds(pl.multiple_of(blocks[e, i] * BLK, BLK), BLK)
                target = slice(i * BLK, (i + 1) * BLK)
                part_hi[slot, target, :] = win_hi[source, :]
                part_lo[slot, target, :] = win_lo[source, :]
            high, low = split(rows[pl.ds(pl.multiple_of(e * BLK, BLK), BLK), :])
            both = dot(jnp.concatenate([high, low], axis=0), part_hi[slot])
            there = pl.ds(pl.multiple_of(g * BLK, BLK), BLK)
            total = both[:BLK] + both[BLK:] + dot(high, part_lo[slot])
            full[there, :] = total * mask[there, :]
        return carry

    lax.fori_loop(0, SLAB // BLK // width, some_blocks, 0)
    send_parts(full[...], parity[0] == 1, own, up, down)


def final_kernel(packed, density, charges):
    half = CHUNK // 2
    first = lax.broadcasted_iota(jnp.int32, (CHUNK, 128), 1) < CHUNK
    total = jnp.zeros((CHUNK, 128), f32)
    for m in range(SLAB // (2 * CHUNK)):
        a, b = packed[2 * m], packed[2 * m + 1]
        ab, bb = a[:CHUNK], b[:CHUNK]
        a2, b2 = a[CHUNK:], b[CHUNK:]
        left = jnp.where(first, ab, pltpu.roll(bb, CHUNK, 1))
        middle = jnp.where(first, pltpu.roll(ab, CHUNK, 1), bb)
        right = jnp.concatenate(
            [
                jnp.where(first[:half], a2, pltpu.roll(b2, CHUNK, 1)),
                jnp.where(first[:half], pltpu.roll(a2, CHUNK, 1), b2),
            ],
            axis=0,
        )
        for j, part in enumerate((left, middle, right)):
            density[:, j * SLAB + m * 128 : j * SLAB + (m + 1) * 128] = part
        total += left + middle + right
    charges[...] = jnp.sum(total.T, axis=0, keepdims=True)


def shards(hamiltonian, root, pattern, sub_blocks, sub_count):
    sds = jax.ShapeDtypeStruct
    slab = lax.axis_index("rows")
    col, core = lax.axis_index("cols"), lax.axis_index("space")
    home = 2 * col + core
    parts = (sds((SLAB, LANES), f32), sds((SLAB, 2 * CHUNK), f32), sds((SLAB, 2 * CHUNK), f32))
    product = dict(flops=6 * SLAB * 3 * SLAB * LANES, moved=6 << 20)

    with jax.named_scope("inputs"):
        chips = jnp.stack([col, (col + 3) % 4, (col + 1) % 4, (col + 2) % 4])
        order = jnp.concatenate([2 * chips + core, 2 * chips + 1 - core]).astype(jnp.int32)
        places = (2 * order[:, None] + jnp.arange(2, dtype=jnp.int32)[None, :]).reshape(-1)
        pieces = [lax.dynamic_slice(root, (0, j * SLAB + home * CHUNK), (SLAB, CHUNK)) for j in range(3)]
        above = passed_along(jnp.concatenate(pieces[1:], axis=1), "rows", 1)
        below = passed_along(jnp.concatenate(pieces[:2], axis=1), "rows", -1)
        odd = slab % 2 == 1
        parity = lax.broadcast_in_dim((slab % 2).astype(jnp.int32), (8,), ())
        ham = around(hamiltonian) + (passed_along(hamiltonian, "cols", 2),)
        own = jnp.concatenate(pieces + [jnp.zeros((SLAB, CHUNK), f32)], axis=1)
        mask = lax.dynamic_slice(pattern, (slab * 16, 0), (16, 48)).astype(f32).reshape(16, 3, 16)
        mask = lax.dynamic_slice(mask, (0, 0, 2 * home), (16, 3, 2)).reshape(16, 6)
        mask = jnp.pad(mask, ((0, 0), (0, 2)))
        mask = jnp.broadcast_to(mask[:, None, :, None], (16, BLK, 8, BLK)).reshape(SLAB, LANES)
        root_hi, root_lo = kernel_call(
            split_kernel,
            (sds((SLAB, 3 * SLAB), bf16),) * 2,
            (root,),
            [VMEM],
            limit=8,
            flops=1 << 22,
            moved=8 << 20,
        )
        chips = jnp.stack([col, (col + 3) % 4, (col + 1) % 4, (col + 2) % 4])
        order = jnp.concatenate([2 * chips + core, 2 * chips + 1 - core]).astype(jnp.int32)
        places = (2 * order[:, None] + jnp.arange(2, dtype=jnp.int32)[None, :]).reshape(-1)
        ready = (above, below, own, mask, root_hi, root_lo, order, places, parity, ham)
        above, below, own, mask, root_hi, root_lo, order, places, parity, ham = lax.optimization_barrier(ready)
        ham = swapped(ham)
    with jax.named_scope("half_done"):
        own, up, down, win_hi, win_lo = kernel_call(
            first_kernel,
            parts + (sds((3 * SLAB, LANES), bf16),) * 2,
            (order, parity) + ham + (above, own, below, mask),
            [SMEM] * 2 + [VMEM] * 12,
            scratch=[pltpu.VMEM((SLAB, 3 * SLAB), bf16)] * 2,
            limit=16,
            **product,
        )
        above, below = met(up), met_after(down)
    with jax.named_scope("orthogonal"):
        mine, up, down = kernel_call(
            ortho_kernel,
            (sds((3 * CHUNK + 8, SLAB), f32),) + (sds((2 * CHUNK, SLAB), f32),) * 2,
            (sub_blocks, parity, root_hi, root_lo, above, own, below, mask),
            [SMEM] * 2 + [VMEM] * 6,
            **product,
        )
        above, below = met(up), met_after(down)
        _, before, after = around(mine)
        far = passed_along(mine, "cols", 2)
        above, before = lax.optimization_barrier((above, before))
        below, after = lax.optimization_barrier((below, after))
        above = around(above) + (met(jnp.where(odd, far[: 2 * CHUNK], far[CHUNK : 3 * CHUNK])),)
        below = around(below) + (passed_along(below, "cols", 2),)
        whole, above = lax.optimization_barrier(((mine, before, after, far), above))
        below = lax.optimization_barrier(below)
        window = swapped(whole) + swapped(above) + swapped(below)
    with jax.named_scope("solve"):
        rows, lists = kernel_call(
            solve_kernel,
            (sds((2 * BLK, ORDER), f32), sds((2 * SLAB // CHUNK, 128), jnp.int32)),
            (sub_blocks, sub_count, order, parity) + window,
            [SMEM] * 4 + [VMEM] * 24,
            scratch=[
                pltpu.SMEM((2, 3 * 16), jnp.int32),
                pltpu.VMEM((2, ORDER + BLK, 3 * SLAB), f32),
                pltpu.VMEM((3 * SLAB, ORDER), f32),
                pltpu.VMEM((2, ORDER, ORDER), f32),
                pltpu.VMEM((8, ORDER), jnp.int32),
            ],
            limit=24,
            flops=12 * ORDER**3,
            moved=8 << 20,
        )
    with jax.named_scope("share"):
        rows = shared(rows)
    with jax.named_scope("half_back"):
        own, up, down = kernel_call(
            back_kernel,
            parts,
            (lists, places, parity) + rows + (win_hi, win_lo, mask),
            [SMEM] * 3 + [VMEM] * 11,
            scratch=[
                pltpu.VMEM((SLAB, ORDER), f32),
                pltpu.VMEM((SLAB, LANES), f32),
                pltpu.VMEM((4, ORDER, LANES), bf16),
                pltpu.VMEM((4, ORDER, LANES), bf16),
            ],
            **product,
        )
        above, below = met(up), met_after(down)
    with jax.named_scope("density"):
        packed = kernel_call(
            density_kernel,
            sds((SLAB // CHUNK, 3 * CHUNK // 2, 2 * CHUNK), f32),
            (parity, root_hi, root_lo, above, own, below, mask),
            [SMEM] + [VMEM] * 6,
            **product,
        )
        packed = lax.all_to_all(packed, ALL, 0, 0)
        density, charges = kernel_call(
            final_kernel,
            (sds((CHUNK, 3 * SLAB), f32), sds((1, CHUNK), f32)),
            (packed,),
            [VMEM],
            flops=1 << 20,
            moved=1 << 20,
        )
    return density, charges.reshape(CHUNK)


def solution(mesh):
    return jax.shard_map(
        shards,
        mesh=mesh,
        in_specs=(
            P(("rows", "cols", "space"), None),
            P("rows", None),
            P(),
            P(("rows", "cols", "space"), None),
            P(("rows", "cols", "space")),
        ),
        out_specs=(P(("rows", "cols", "space"), None), P(("rows", "cols", "space"))),
        check_vma=False,
    )
```

```python
import functools

import jax
import jax.numpy as jnp
from jax import lax
from jax.experimental import pallas as pl
from jax.experimental.pallas import tpu as pltpu
from jax.sharding import PartitionSpec as P

BLK = 32
MAXB = 16
SLAB = 512
CHUNK = 64
LANES = 256
ORDER = MAXB * BLK
f32 = jnp.float32
bf16 = jnp.bfloat16
ALL = ("cols", "space")
VMEM = pl.BlockSpec(memory_space=pltpu.VMEM)
SMEM = pl.BlockSpec(memory_space=pltpu.SMEM)


def passed_along(value, axis, steps):
    count = lax.axis_size(axis)
    pairs = [(source, (source + steps) % count) for source in range(count)]
    return lax.ppermute(value, axis, pairs)


def around(value):
    return value, passed_along(value, "cols", 1), passed_along(value, "cols", -1)


def swapped(values):
    return values + tuple(passed_along(value, "space", 1) for value in values)


def shared(value):
    return swapped(around(value) + (passed_along(value, "cols", 2),))


def kernel_call(body, shapes, operands, in_specs, scratch=(), limit=12, flops=0, moved=0):
    return pl.pallas_call(
        body,
        out_shape=shapes,
        in_specs=in_specs,
        out_specs=jax.tree.map(lambda _: VMEM, shapes),
        scratch_shapes=list(scratch),
        compiler_params=pltpu.CompilerParams(vmem_limit_bytes=limit << 20),
        cost_estimate=pl.CostEstimate(flops=flops, bytes_accessed=moved, transcendentals=0),
    )(*operands)


def split(x):
    high = x.astype(bf16)
    return high, (x - high.astype(f32)).astype(bf16)


def dot3(a, b):
    dot = functools.partial(jnp.dot, preferred_element_type=f32)
    return dot(a[0], b[0]) + (dot(a[0], b[1]) + dot(a[1], b[0]))


def send_parts(full, own, up, down):
    own[...] = full
    up[...] = pltpu.roll(full, LANES - CHUNK, 1)[:, : 2 * CHUNK]
    down[...] = full[:, : 2 * CHUNK]


def window_parts(above, own, below):
    blank = jnp.zeros((SLAB, 2 * CHUNK), f32)
    return (
        jnp.concatenate([above, blank], axis=1),
        own,
        pltpu.roll(jnp.concatenate([below, blank], axis=1), CHUNK, 1),
    )


def split_kernel(root, root_hi, root_lo):
    root_hi[...], root_lo[...] = split(root[...])


def first_kernel(order, *refs):
    pieces, refs = refs[:8], refs[8:]
    above, mine, below, mask, own, up, down, win_hi, win_lo, ham_hi, ham_lo = refs
    for k, part in enumerate(window_parts(above[...], mine[...], below[...])):
        cut = slice(k * SLAB, (k + 1) * SLAB)
        win_hi[cut, :], win_lo[cut, :] = split(part)
    for n, piece in enumerate(pieces):
        there = pl.ds(pl.multiple_of(order[n] * CHUNK, CHUNK), CHUNK)
        ham_hi[there, :], ham_lo[there, :] = split(piece[...])
    total = jnp.zeros((SLAB, LANES), f32)
    for k in range(3):
        cut = slice(k * SLAB, (k + 1) * SLAB)
        total += dot3((ham_hi[:, cut], ham_lo[:, cut]), (win_hi[cut, :], win_lo[cut, :]))
    send_parts(total * mask[...], own, up, down)


def root_product(root_hi, root_lo, above, own, below, mask):
    total = jnp.zeros((SLAB, LANES), f32)
    for k, part in enumerate(window_parts(above[...], own[...], below[...])):
        cut = slice(k * SLAB, (k + 1) * SLAB)
        total += dot3((root_hi[:, cut], root_lo[:, cut]), split(part))
    return total * mask[...]


def ortho_kernel(blocks, root_hi, root_lo, above, own, below, mask, mine, up, down):
    turned = root_product(root_hi, root_lo, above, own, below, mask).T
    mine[: 3 * CHUNK, :] = turned[: 3 * CHUNK]
    up[...] = turned[CHUNK : 3 * CHUNK]
    down[...] = turned[: 2 * CHUNK]
    line = lax.broadcasted_iota(jnp.int32, (8, SLAB), 0)
    lane = lax.broadcasted_iota(jnp.int32, (8, SLAB), 1)
    lists = jnp.zeros((8, SLAB), jnp.int32)
    for g in range(2):
        for i in range(MAXB):
            lists = jnp.where((line == g) & (lane == i), blocks[g, i], lists)
    mine[3 * CHUNK :, :] = lists.astype(f32)


def density_kernel(root_hi, root_lo, above, own, below, mask, packed):
    full = root_product(root_hi, root_lo, above, own, below, mask)
    half = CHUNK // 2
    for c in range(SLAB // CHUNK):
        rows = full[c * CHUNK : (c + 1) * CHUNK]
        packed[c, :CHUNK, :] = rows[:, : 2 * CHUNK]
        last = rows[:, 2 * CHUNK :]
        lane = lax.broadcasted_iota(jnp.int32, (half, 2 * CHUNK), 1)
        packed[c, CHUNK:, :] = jnp.where(lane < CHUNK, last[:half], pltpu.roll(last[half:], CHUNK, 1))


def solve_kernel(blocks, counts, order, *refs):
    pieces, (out, lists, inverse, rows, turned, assembled, valid) = refs[:24], refs[24:]
    row_id = lax.broadcasted_iota(jnp.int32, (BLK, ORDER), 0)
    col_id = lax.broadcasted_iota(jnp.int32, (BLK, ORDER), 1)
    list_id = lax.broadcasted_iota(jnp.int32, (1, ORDER), 1) // BLK
    dot = functools.partial(jnp.dot, preferred_element_type=f32)

    for g in range(2):
        for q in range(3 * 16):
            inverse[g, q] = MAXB
        for k in range(MAXB):
            inverse[g, blocks[g, k]] = k
    for n in range(8):
        lists[2 * n : 2 * n + 2, :] = pieces[n][3 * CHUNK : 3 * CHUNK + 2, :128].astype(jnp.int32)
        for panel, piece, first in ((1, pieces[n], 0), (0, pieces[8 + n], 0), (2, pieces[16 + n], 1)):
            for at in range(6 if panel == 1 else 4):
                q = (first + at // 2) * 16 + 2 * order[n] + at % 2
                block = piece[at * BLK : (at + 1) * BLK, :]
                for g in range(2):
                    there = pl.ds(pl.multiple_of(inverse[g, q] * BLK, BLK), BLK)
                    rows[g, there, panel * SLAB : (panel + 1) * SLAB] = block

    def gather(g):
        for panel in range(3):
            flags = jnp.zeros((1, ORDER), jnp.int32)
            for k in range(MAXB):
                keep = (k < counts[g]) & (jnp.abs(blocks[g, k] // 16 - panel) <= 1)
                flags = jnp.where(list_id == k, jnp.where(keep, 1, 0), flags)
            valid[panel : panel + 1, :] = flags
            cut = slice(panel * SLAB, (panel + 1) * SLAB)
            turned[cut, :] = rows[g, :ORDER, cut].T

        def one_column(k, carry):
            p = blocks[g, k]
            there = pl.ds(pl.multiple_of(k * BLK, BLK), BLK)
            source = pl.ds(pl.multiple_of(p * BLK, BLK), BLK)
            keep = valid[pl.ds(p // 16, 1), :] + jnp.where(k < counts[g], 0, -1) > 0
            assembled[g, there, :] = jnp.where(keep, turned[source, :], 0.0)
            return carry

        lax.fori_loop(0, MAXB, one_column, 0, unroll=4)

    def scaled(g):
        whole_block = assembled[g]
        symmetric = 0.5 * (whole_block + whole_block.T)
        squares = jnp.sum(symmetric * symmetric, keepdims=True) + 1e-06
        size = jnp.full((1, 1), counts[g] * BLK, jnp.int32).astype(f32)
        return symmetric * (jnp.sqrt(size) / (2.0 * jnp.sqrt(squares)))

    def thin(home, parts):
        high, low = split(home)
        both = dot(jnp.concatenate([high, low], axis=0), parts[0])
        return both[:BLK] + both[BLK:] + dot(high, parts[1])

    for g in range(2):
        gather(g)
    iterates = [scaled(g) for g in range(2)]
    squares = [split(dot3(parts, parts)) for parts in [split(iterate) for iterate in iterates]]
    firsts = [iterate[:BLK] for iterate in iterates]
    firsts = [1.5 * first - 0.5 * thin(first, square) for first, square in zip(firsts, squares)]
    cubes = [thin(first, square) for first, square in zip(firsts, squares)]
    for _ in range(2):
        cubes = [1.5 * cube - 0.5 * thin(cube, square) for cube, square in zip(cubes, squares)]
    for g in range(2):
        home = 1.5 * firsts[g] - 0.5 * cubes[g]
        out[g * BLK : (g + 1) * BLK, :] = 0.5 * (jnp.where(row_id == col_id, 1.0, 0.0) - home)


def back_kernel(blocks, places, *refs):
    pieces, (win_hi, win_lo, mask, own, up, down, rows, full, part_hi, part_lo) = refs[:8], refs[8:]
    for n, piece in enumerate(pieces):
        rows[n * 2 * BLK : (n + 1) * 2 * BLK, :] = piece[...]
    dot = functools.partial(jnp.dot, preferred_element_type=f32)
    width = part_hi.shape[0]

    def some_blocks(step, carry):
        for slot in range(width):
            e = step * width + slot
            g = places[e]
            for i in range(MAXB):
                source = pl.ds(pl.multiple_of(blocks[e, i] * BLK, BLK), BLK)
                target = slice(i * BLK, (i + 1) * BLK)
                part_hi[slot, target, :] = win_hi[source, :]
                part_lo[slot, target, :] = win_lo[source, :]
            high, low = split(rows[pl.ds(pl.multiple_of(e * BLK, BLK), BLK), :])
            both = dot(jnp.concatenate([high, low], axis=0), part_hi[slot])
            there = pl.ds(pl.multiple_of(g * BLK, BLK), BLK)
            total = both[:BLK] + both[BLK:] + dot(high, part_lo[slot])
            full[there, :] = total * mask[there, :]
        return carry

    lax.fori_loop(0, SLAB // BLK // width, some_blocks, 0)
    send_parts(full[...], own, up, down)


def final_kernel(packed, density, charges):
    half = CHUNK // 2
    first = lax.broadcasted_iota(jnp.int32, (CHUNK, 128), 1) < CHUNK
    total = jnp.zeros((CHUNK, 128), f32)
    for m in range(SLAB // (2 * CHUNK)):
        a, b = packed[2 * m], packed[2 * m + 1]
        ab, bb = a[:CHUNK], b[:CHUNK]
        a2, b2 = a[CHUNK:], b[CHUNK:]
        left = jnp.where(first, ab, pltpu.roll(bb, CHUNK, 1))
        middle = jnp.where(first, pltpu.roll(ab, CHUNK, 1), bb)
        right = jnp.concatenate(
            [
                jnp.where(first[:half], a2, pltpu.roll(b2, CHUNK, 1)),
                jnp.where(first[:half], pltpu.roll(a2, CHUNK, 1), b2),
            ],
            axis=0,
        )
        for j, part in enumerate((left, middle, right)):
            density[:, j * SLAB + m * 128 : j * SLAB + (m + 1) * 128] = part
        total += left + middle + right
    charges[...] = jnp.sum(total.T, axis=0, keepdims=True)


def shards(hamiltonian, root, pattern, sub_blocks, sub_count):
    sds = jax.ShapeDtypeStruct
    slab = lax.axis_index("rows")
    col, core = lax.axis_index("cols"), lax.axis_index("space")
    home = 2 * col + core
    parts = (sds((SLAB, LANES), f32), sds((SLAB, 2 * CHUNK), f32), sds((SLAB, 2 * CHUNK), f32))
    product = dict(flops=6 * SLAB * 3 * SLAB * LANES, moved=6 << 20)

    with jax.named_scope("inputs"):
        chips = jnp.stack([col, (col + 3) % 4, (col + 1) % 4, (col + 2) % 4])
        order = jnp.concatenate([2 * chips + core, 2 * chips + 1 - core]).astype(jnp.int32)
        places = (2 * order[:, None] + jnp.arange(2, dtype=jnp.int32)[None, :]).reshape(-1)
        pieces = [lax.dynamic_slice(root, (0, j * SLAB + home * CHUNK), (SLAB, CHUNK)) for j in range(3)]
        above = passed_along(jnp.concatenate(pieces[1:], axis=1), "rows", 1)
        below = passed_along(jnp.concatenate(pieces[:2], axis=1), "rows", -1)
        ham = around(hamiltonian) + (passed_along(hamiltonian, "cols", 2),)
        own = jnp.concatenate(pieces + [jnp.zeros((SLAB, CHUNK), f32)], axis=1)
        mask = lax.dynamic_slice(pattern, (slab * 16, 0), (16, 48)).astype(f32).reshape(16, 3, 16)
        mask = lax.dynamic_slice(mask, (0, 0, 2 * home), (16, 3, 2)).reshape(16, 6)
        mask = jnp.pad(mask, ((0, 0), (0, 2)))
        mask = jnp.broadcast_to(mask[:, None, :, None], (16, BLK, 8, BLK)).reshape(SLAB, LANES)
        root_hi, root_lo = kernel_call(
            split_kernel,
            (sds((SLAB, 3 * SLAB), bf16),) * 2,
            (root,),
            [VMEM],
            limit=8,
            flops=1 << 22,
            moved=8 << 20,
        )
        chips = jnp.stack([col, (col + 3) % 4, (col + 1) % 4, (col + 2) % 4])
        order = jnp.concatenate([2 * chips + core, 2 * chips + 1 - core]).astype(jnp.int32)
        places = (2 * order[:, None] + jnp.arange(2, dtype=jnp.int32)[None, :]).reshape(-1)
        ready = (above, below, own, mask, root_hi, root_lo, order, places, ham)
        above, below, own, mask, root_hi, root_lo, order, places, ham = lax.optimization_barrier(ready)
        ham = swapped(ham)
    with jax.named_scope("half_done"):
        own, up, down, win_hi, win_lo = kernel_call(
            first_kernel,
            parts + (sds((3 * SLAB, LANES), bf16),) * 2,
            (order,) + ham + (above, own, below, mask),
            [SMEM] + [VMEM] * 12,
            scratch=[pltpu.VMEM((SLAB, 3 * SLAB), bf16)] * 2,
            limit=16,
            **product,
        )
        above, below = passed_along(up, "rows", 1), passed_along(down, "rows", -1)
    with jax.named_scope("orthogonal"):
        mine, up, down = kernel_call(
            ortho_kernel,
            (sds((3 * CHUNK + 8, SLAB), f32),) + (sds((2 * CHUNK, SLAB), f32),) * 2,
            (sub_blocks, root_hi, root_lo, above, own, below, mask),
            [SMEM] + [VMEM] * 6,
            **product,
        )
        above, below = passed_along(up, "rows", 1), passed_along(down, "rows", -1)
        _, before, after = around(mine)
        far = passed_along(mine, "cols", 2)
        above, below, before, after = lax.optimization_barrier((above, below, before, after))
        above = around(above) + (passed_along(far[CHUNK : 3 * CHUNK], "rows", 1),)
        below = around(below) + (passed_along(below, "cols", 2),)
        whole, above = lax.optimization_barrier(((mine, before, after, far), above))
        below = lax.optimization_barrier(below)
        window = swapped(whole) + swapped(above) + swapped(below)
    with jax.named_scope("solve"):
        rows, lists = kernel_call(
            solve_kernel,
            (sds((2 * BLK, ORDER), f32), sds((2 * SLAB // CHUNK, 128), jnp.int32)),
            (sub_blocks, sub_count, order) + window,
            [SMEM] * 3 + [VMEM] * 24,
            scratch=[
                pltpu.SMEM((2, 3 * 16), jnp.int32),
                pltpu.VMEM((2, ORDER + BLK, 3 * SLAB), f32),
                pltpu.VMEM((3 * SLAB, ORDER), f32),
                pltpu.VMEM((2, ORDER, ORDER), f32),
                pltpu.VMEM((8, ORDER), jnp.int32),
            ],
            limit=24,
            flops=12 * ORDER**3,
            moved=8 << 20,
        )
    with jax.named_scope("share"):
        rows = shared(rows)
    with jax.named_scope("half_back"):
        own, up, down = kernel_call(
            back_kernel,
            parts,
            (lists, places) + rows + (win_hi, win_lo, mask),
            [SMEM, SMEM] + [VMEM] * 11,
            scratch=[
                pltpu.VMEM((SLAB, ORDER), f32),
                pltpu.VMEM((SLAB, LANES), f32),
                pltpu.VMEM((4, ORDER, LANES), bf16),
                pltpu.VMEM((4, ORDER, LANES), bf16),
            ],
            **product,
        )
        above, below = passed_along(up, "rows", 1), passed_along(down, "rows", -1)
    with jax.named_scope("density"):
        packed = kernel_call(
            density_kernel,
            sds((SLAB // CHUNK, 3 * CHUNK // 2, 2 * CHUNK), f32),
            (root_hi, root_lo, above, own, below, mask),
            [VMEM] * 6,
            **product,
        )
        packed = lax.all_to_all(packed, ALL, 0, 0)
        density, charges = kernel_call(
            final_kernel,
            (sds((CHUNK, 3 * SLAB), f32), sds((1, CHUNK), f32)),
            (packed,),
            [VMEM],
            flops=1 << 20,
            moved=1 << 20,
        )
    return density, charges.reshape(CHUNK)


def solution(mesh):
    return jax.shard_map(
        shards,
        mesh=mesh,
        in_specs=(
            P(("rows", "cols", "space"), None),
            P("rows", None),
            P(),
            P(("rows", "cols", "space"), None),
            P(("rows", "cols", "space")),
        ),
        out_specs=(P(("rows", "cols", "space"), None), P(("rows", "cols", "space"))),
        check_vma=False,
    )
```
